32 devices in a mesh: dp: 2 (over x), fsdp: 4 (over z), expert: 4 (over y, core).
Axes of the slice: x: 2, y: 2, z: 4, core: 2. Of those that a mesh axis runs over, the one named last changes fastest.
Arguments:
- window: bfloat16 [256, 4096], P('fsdp'), may hold values from -3 to 3
- attention_gain: float32 [4096], replicated, may hold values from 0.1 to 1.9
- query_weight: bfloat16 [4096, 4096], P('fsdp', 'expert'), may hold values from -0.09375 to 0.09375
- key_weight: bfloat16 [4096, 1024], P('fsdp', 'expert'), may hold values from -0.1875 to 0.1875
- value_weight: bfloat16 [4096, 1024], P('fsdp', 'expert'), may hold values from -0.1875 to 0.1875
- out_weight: bfloat16 [4096, 4096], P('expert', 'fsdp'), may hold values from -0.1875 to 0.1875
- cache_keys: bfloat16 [1024, 1024], P('dp', 'expert'), may hold values from -104 to 104
- cache_values: bfloat16 [1024, 1024], P('dp', 'expert'), may hold values from -12 to 12
- occluded: int32 [1024, 2], P('dp'), may hold values from 0 to 1, as said below
- feedforward_gain: float32 [4096], replicated, may hold values from 0.1 to 1.9
- router_weight: bfloat16 [4096, 4], replicated, may hold values from -0.0234375 to 0.0234375
- chosen_experts: int32 [2, 256, 2], P('dp', 'fsdp'), may hold values from 0 to 3, all different within a row; in each aligned block of 64 rows (0 to 63, 64 to 127, ..., all dimensions but the last counted through in order) at most 64 rows name the same one
- gate_weight: bfloat16 [4, 12288, 4096], P('expert', ('dp', 'fsdp')), may hold values from -0.09375 to 0.09375
- up_weight: bfloat16 [4, 12288, 4096], P('expert', ('dp', 'fsdp')), may hold values from -0.09375 to 0.09375
- down_weight: bfloat16 [4, 12288, 4096], P('expert', ('dp', 'fsdp')), may hold values from -0.0546875 to 0.0546875
Outputs:
- layer_output: bfloat16 [2, 256, 4096], P('dp', 'fsdp')
The draws below stay inside these ranges and needn't reach their ends.
Inputs may be any that keep to these rules, and one draw needn't show every extreme that they name: `chosen_experts`: each row names 2 different experts. In each aligned block of 64 rows, counting the leading dimensions together (the rows of one device), no expert is named by more than 64 rows, a bound that some block reaches. `occluded`: constant over each aligned run of 64 prefix positions.
All inputs are finite; a program needn't handle non-finite values.
Results may differ from the reference program's by a relative error of at most 0.0095.
The reference program's roundings to bfloat16 on the way count: a program that leaves them out, or rounds other values in their place, can miss the bound.
Values may be sent and summed in bfloat16 or wider, within the bound.
A program may use at most 128 MiB of HBM per device.

```python
import math
import jax
import jax.numpy as jnp
import numpy as np
from jax import lax

D = 4096
H = 32
KVH = 8
HD = 128
FF = 12288
TOP = 2
TOK_DEV = 64
EXPERTS = 4
WINDOW = 256
PREFIX = 1024
VARIANTS = 2
SECTION = 64
CAP = 64
N_DP = 2
N_FSDP = 4


def draw_cache_keys(key, part):
    extent = (PREFIX, KVH * HD)
    return (2.0 * jax.random.truncated_normal(key, -6.0, 6.0, extent, jnp.float32)).astype(jnp.bfloat16)


def draw_occluded(key, part):
    section_count = PREFIX // SECTION
    coin_rolls = jax.random.randint(key, (section_count, VARIANTS), 0, 8)
    covered = (coin_rolls < 3).astype(jnp.int32)
    return jnp.repeat(covered, SECTION, axis=0)


def block_levels(stream_key, shape, shards, low, top_value):
    gain = 1.0
    for axis_at, parts in shards:
        draws = jax.random.uniform(jax.random.fold_in(jax.random.fold_in(stream_key, 6), axis_at), (parts,), jnp.float32, low / len(shards), top_value / len(shards))
        gain = gain * jnp.repeat(jnp.exp(draws), shape[axis_at] // parts).reshape((-1,) + (1,) * (len(shape) - 1 - axis_at))
    return gain


def deal_out(rng, own, number, rows, number_of, top, most, skew):
    sequence = jax.random.permutation(rng, number_of)
    heavy_load, usual = portions_of(number_of, rows * top, most, skew, True), portions_of(number_of, rows * top, most, skew, False)
    places = jnp.arange(number_of)

    def named(lengths, offset_by):
        used = int((lengths > 0).sum())
        fixed = max(1, used // 4)
        shifted = fixed + (places - fixed + offset_by * (used - fixed)) % max(1, number_of - fixed)
        return jnp.zeros((number_of,), jnp.int32).at[sequence[jnp.where(places < fixed, places, shifted)]].set(jnp.asarray(lengths, jnp.int32))

    lengths = jnp.where(number % 4 == 0, named(heavy_load, number // 4), named(usual, number - number // 4 - 1))
    mixed = jax.random.permutation(jax.random.fold_in(own, 3), number_of)
    donor, receiver = mixed[0:number_of // 2 * 2:2], mixed[1:number_of // 2 * 2:2]
    room = jnp.minimum(lengths[donor] - 1, most - lengths[receiver]) // 2
    room = jnp.where((donor == sequence[0]) | (receiver == sequence[0]) | (lengths[receiver] == 0), 0, jnp.maximum(room, 0))
    shifted = jax.random.randint(jax.random.fold_in(own, 4), (number_of // 2,), 0, 1 << 20) % (room + 1)
    lengths = lengths.at[donor].add(-shifted).at[receiver].add(shifted)
    items = jnp.searchsorted(jnp.cumsum(lengths), jnp.arange(rows * top), side="right").astype(jnp.int32)
    listing = items.reshape(top, rows).T
    listing = listing[jax.random.permutation(jax.random.fold_in(own, 1), rows)]
    offset_by = jax.random.randint(jax.random.fold_in(own, 2), (rows, 1), 0, top)
    return jnp.take_along_axis(listing, (jnp.arange(top)[None, :] + offset_by) % top, axis=1)


def portions_of(number_of, total, most, slope, full):
    weights = [(1 << 20) // math.isqrt(rank ** slope) + 1 for rank in range(1, number_of + 1)]
    largest = most if full else min(most, max(-(-total // number_of), total * weights[0] // sum(weights)))
    least = 1 if total - largest >= number_of - 1 else 0
    counts, spare = [largest] + [least] * (number_of - 1), total - largest - least * (number_of - 1)
    while spare > 0:
        candidates = [i for i in range(1, number_of) if counts[i] < largest] or [i for i in range(1, number_of) if counts[i] < most]
        whole, left = sum([weights[i] for i in candidates]), spare
        for i in candidates:
            addition = min(most - counts[i], max(1, left * weights[i] // whole), spare)
            counts[i] = counts[i] + addition
            spare = spare - addition
    return np.array(counts)


def gaussian(stream_key, shape, scale, most, cuts=(), kind=jnp.bfloat16):
    factor_of = block_levels(stream_key, shape, cuts, -0.22, 0.18) if cuts else 1.0
    entries = jax.random.normal(stream_key, shape, jnp.float32) * scale * factor_of
    return jnp.minimum(jnp.maximum(entries, -most), most).astype(kind)


def setup_inputs(seed: int = 0) -> dict:
    keys = jax.random.split(jax.random.key(seed), 16)
    window = gaussian(keys[0], (WINDOW, D), 0.5, 3.0, ((0, 4),))
    attention_gain = jnp.clip(1.0 + 0.18 * jax.random.normal(keys[1], (D,), jnp.float32), 0.1, 1.9)
    query_weight = gaussian(keys[2], (D, H * HD), D ** -0.5, 0.09375, ((0, 4), (1, 4)))
    key_weight = gaussian(keys[3], (D, KVH * HD), (D // 4) ** -0.5, 0.1875, ((0, 4), (1, 4)))
    value_weight = gaussian(keys[4], (D, KVH * HD), (D // 4) ** -0.5, 0.1875, ((0, 4), (1, 4)))
    out_weight = gaussian(keys[5], (H * HD, D), (H * HD // 4) ** -0.5, 0.1875, ((0, 4), (1, 4)))
    cache_keys = draw_cache_keys(jax.random.fold_in(keys[15], 71), 0)
    cache_values = gaussian(keys[7], (PREFIX, KVH * HD), 2.0, 12.0, ((0, 2), (1, 4)))
    occluded = draw_occluded(jax.random.fold_in(keys[15], 71), 0)
    feedforward_gain = jnp.clip(1.0 + 0.18 * jax.random.normal(keys[9], (D,), jnp.float32), 0.1, 1.9)
    router_weight = gaussian(keys[10], (D, EXPERTS), (16 * D) ** -0.5, 0.0234375)
    chosen_experts_keys = jax.random.split(jax.random.fold_in(keys[11], 1), VARIANTS * WINDOW // TOK_DEV)
    chosen_experts_turns = jax.random.permutation(jax.random.fold_in(keys[11], 3), VARIANTS * WINDOW // TOK_DEV)
    chosen_experts = jax.vmap(lambda own, number: deal_out(jax.random.fold_in(keys[11], 2), own, number, TOK_DEV, EXPERTS, TOP, CAP, 2))(chosen_experts_keys, chosen_experts_turns).reshape((VARIANTS, WINDOW, TOP))
    gate_weight = gaussian(keys[12], (EXPERTS, FF, D), D ** -0.5, 0.09375, ((0, 4), (1, 8)))
    up_weight = gaussian(keys[13], (EXPERTS, FF, D), D ** -0.5, 0.09375, ((0, 4), (1, 8)))
    down_weight = gaussian(keys[14], (EXPERTS, FF, D), FF ** -0.5, 0.0546875, ((0, 4), (1, 8)))
    return dict(window=window, attention_gain=attention_gain, query_weight=query_weight, key_weight=key_weight, value_weight=value_weight, out_weight=out_weight, cache_keys=cache_keys, cache_values=cache_values, occluded=occluded, feedforward_gain=feedforward_gain, router_weight=router_weight, chosen_experts=chosen_experts, gate_weight=gate_weight, up_weight=up_weight, down_weight=down_weight)


epsilon = 1e-05
rope_base = 1000000.0
floor_score = -1e+30

def rms_norm(values, scales):
    widened = values.astype(jnp.float32)
    inverse = lax.rsqrt(lax.optimization_barrier(jnp.mean(widened * widened, axis=-1, keepdims=True)) + epsilon)
    return (widened * inverse * scales.astype(jnp.float32)).astype(jnp.bfloat16)

def rotate(vectors, positions):
    halfway = vectors.shape[-1] // 2
    powers = jnp.arange(halfway, dtype=jnp.float32) * (2.0 / vectors.shape[-1])
    frequency = rope_base ** (-powers)
    angles = positions.astype(jnp.float32)[:, None] * frequency[None, :]
    cosine = jnp.cos(angles)[:, None, :]
    sine_part = jnp.sin(angles)[:, None, :]
    former = vectors[..., :halfway]
    latter = vectors[..., halfway:]
    return jnp.concatenate([former * cosine - latter * sine_part, latter * cosine + former * sine_part], axis=-1)

def barrier_widen(values):
    return lax.optimization_barrier(values).astype(jnp.float32)

def reference(window, attention_gain, query_weight, key_weight, value_weight, out_weight, cache_keys, cache_values, occluded, feedforward_gain, router_weight, chosen_experts, gate_weight, up_weight, down_weight):
    grouping = H // KVH
    score_scale = HD ** (-0.5)
    normed = rms_norm(window, attention_gain)
    fresh_positions = PREFIX + jnp.arange(WINDOW, dtype=jnp.int32)
    queries = jnp.dot(normed, query_weight, preferred_element_type=jnp.float32).reshape(WINDOW, H, HD)
    queries = rotate(queries, fresh_positions).astype(jnp.bfloat16).reshape(WINDOW, KVH, grouping, HD)
    fresh_keys = jnp.dot(normed, key_weight, preferred_element_type=jnp.float32).reshape(WINDOW, KVH, HD)
    fresh_keys = rotate(fresh_keys, fresh_positions).astype(jnp.bfloat16)
    fresh_values = jnp.dot(normed, value_weight, preferred_element_type=jnp.float32).astype(jnp.bfloat16).reshape(WINDOW, KVH, HD)
    cached_keys = cache_keys.reshape(PREFIX, KVH, HD)
    cached_values = cache_values.reshape(PREFIX, KVH, HD)
    queries_wide = barrier_widen(queries)
    prefix_scores = jnp.einsum('tkgd,pkd->kgtp', queries_wide, cached_keys.astype(jnp.float32)) * score_scale
    window_scores = jnp.einsum('tkgd,jkd->kgtj', queries_wide, barrier_widen(fresh_keys)) * score_scale
    causal = jnp.arange(WINDOW)[None, :] <= jnp.arange(WINDOW)[:, None]
    window_masked = jnp.where(causal, window_scores, floor_score)
    window_top = lax.optimization_barrier(jnp.max(window_masked, axis=-1))
    values_wide = barrier_widen(fresh_values)
    cached_wide = cached_values.astype(jnp.float32)

    def one_variant(visible):
        prefix_masked = jnp.where(visible, prefix_scores, floor_score)
        row_top = jnp.maximum(lax.optimization_barrier(jnp.max(prefix_masked, axis=-1)), window_top)
        prefix_weights = jnp.where(visible, jnp.exp(prefix_masked - row_top[..., None]), 0.0)
        window_weights = jnp.where(causal, jnp.exp(window_masked - row_top[..., None]), 0.0)
        totals = lax.optimization_barrier(jnp.sum(prefix_weights, axis=-1)) + lax.optimization_barrier(jnp.sum(window_weights, axis=-1))
        mixed_values = jnp.einsum('kgtp,pkd->kgtd', barrier_widen(prefix_weights.astype(jnp.bfloat16)), cached_wide)
        mixed_values = mixed_values + jnp.einsum('kgtj,jkd->kgtd', barrier_widen(window_weights.astype(jnp.bfloat16)), values_wide)
        head_values = (mixed_values / totals[..., None]).astype(jnp.bfloat16)
        merged = head_values.transpose(2, 0, 1, 3).reshape(WINDOW, H * HD)
        return window.astype(jnp.float32) + jnp.dot(merged, out_weight, preferred_element_type=jnp.float32)
    residual = lax.map(one_variant, occluded.T == 0)
    groups = N_DP * N_FSDP
    token_count = VARIANTS * WINDOW
    flattened = residual.reshape(token_count, D)
    normed_mix = rms_norm(flattened, feedforward_gain)
    logits = jnp.dot(normed_mix, router_weight, preferred_element_type=jnp.float32)
    expert_picks = chosen_experts.reshape(token_count, TOP)
    picked = jnp.take_along_axis(logits, expert_picks, axis=1)
    gate_shares = jax.nn.sigmoid(picked - picked[:, ::-1])
    shard_count = N_DP * N_FSDP
    shard_width = FF // shard_count
    group_base = jnp.arange(groups, dtype=jnp.int32)[:, None] * CAP
    contract_last = (((1,), (1,)), ((), ()))

    def one_expert(running, inputs):
        expert, gate_rows, up_rows, down_rows = inputs
        expert_hits = expert_picks == expert
        taken_flag = jnp.any(expert_hits, axis=1).astype(jnp.int32)
        weight_mine = lax.optimization_barrier(jnp.sum(jnp.where(expert_hits, gate_shares, 0.0), axis=1))
        blocked = taken_flag.reshape(groups, TOK_DEV)
        slot_numbers = jnp.cumsum(blocked, axis=1) - blocked
        targets = (group_base + slot_numbers).reshape(token_count).astype(jnp.int32)
        targets = jnp.where(taken_flag == 1, targets, groups * CAP).astype(jnp.int32)
        buffer = jnp.zeros((groups * CAP, D), jnp.bfloat16).at[targets].set(normed_mix, mode='drop')
        gate_values = lax.dot_general(buffer, gate_rows, contract_last, preferred_element_type=jnp.float32)
        lifted = lax.dot_general(buffer, up_rows, contract_last, preferred_element_type=jnp.float32)
        hidden = (jax.nn.silu(gate_values) * lifted).astype(jnp.bfloat16)
        hidden_shards = hidden.reshape(groups * CAP, shard_count, shard_width).transpose(1, 0, 2)
        down_shards = down_rows.reshape(shard_count, shard_width, D)

        def add_shard(summed, paired):
            partial_sum = jnp.dot(paired[0], paired[1], preferred_element_type=jnp.float32).astype(jnp.bfloat16)
            return (summed + barrier_widen(partial_sum), None)
        expert_output, unused = lax.scan(add_shard, jnp.zeros((groups * CAP, D), jnp.float32), (hidden_shards, down_shards))
        gathered = expert_output[jnp.minimum(targets, groups * CAP - 1)]
        return (running + gathered * weight_mine[:, None], None)
    mixture, unused = lax.scan(one_expert, jnp.zeros((token_count, D), jnp.float32), (jnp.arange(EXPERTS, dtype=jnp.int32), gate_weight, up_weight, down_weight))
    layer_output = (flattened + mixture).astype(jnp.bfloat16).reshape(VARIANTS, WINDOW, D)
    return layer_output
```

```python
import functools

import jax
import jax.numpy as jnp
from jax import lax
from jax.experimental import pallas as pl
from jax.experimental.pallas import tpu as pltpu
from jax.sharding import PartitionSpec as P

HD = 128
TOP = 2

epsilon = 1e-05
rope_base = 1000000.0
floor_score = -1e30
MESH = pl.DeviceIdType.MESH


def rms_norm(values, scales):
    widened = values.astype(jnp.float32)
    inverse = lax.rsqrt(jnp.mean(widened * widened, axis=-1, keepdims=True) + epsilon)
    return (widened * inverse * scales).astype(jnp.bfloat16)


def rotate(vectors, positions):
    halfway = vectors.shape[-1] // 2
    powers = jnp.arange(halfway, dtype=jnp.float32) * (2.0 / vectors.shape[-1])
    frequency = rope_base ** (-powers)
    angles = positions.astype(jnp.float32)[:, None] * frequency[None, :]
    cosine = jnp.cos(angles)[:, None, :]
    sine_part = jnp.sin(angles)[:, None, :]
    former = vectors[..., :halfway]
    latter = vectors[..., halfway:]
    return jnp.concatenate(
        [former * cosine - latter * sine_part, latter * cosine + former * sine_part], axis=-1
    )


def linear_place(axes, sizes):
    place = 0
    for axis in axes:
        place = place * sizes[axis] + lax.axis_index(axis)
    return place


def coordinates(axes, sizes, place):
    found = {}
    for axis in reversed(axes):
        found[axis] = lax.rem(place, sizes[axis])
        place = place // sizes[axis]
    return found


def count(axes, sizes):
    total = 1
    for axis in axes:
        total *= sizes[axis]
    return total


def source_part(kind, ref, to):
    if kind == "gather":
        return ref
    if kind == "rows":
        return ref.at[to]
    if kind == "second":
        return ref.at[:, to]
    if kind == "rows_to_columns":
        return ref.at[to]
    raise ValueError(kind)


def exchange_kernel(kinds, sizes, *refs):
    n = len(kinds)
    inputs, outputs, sems = refs[:n], refs[n : 2 * n], refs[2 * n :]
    barrier = pltpu.get_barrier_semaphore()
    total = 0
    for _, axes in kinds:
        size = count(axes, sizes)
        here = linear_place(axes, sizes)
        for k in range(1, size):
            to = coordinates(axes, sizes, lax.rem(here + k, size))
            pl.semaphore_signal(barrier, inc=1, device_id=to, device_id_type=MESH)
        total += size - 1
    local_copies = []

    def landing(kind, out, here, width):
        if kind == "rows_to_columns":
            return out.at[:, pl.ds(pl.multiple_of(here * width, 128), width)]
        return out.at[here]

    def part(kind, ref, to, size):
        if kind == "columns":
            width = ref.shape[1] // size
            return ref.at[:, pl.ds(pl.multiple_of(to * width, 128), width)]
        return source_part(kind, ref, to)

    for i, (kind, axes) in enumerate(kinds):
        size = count(axes, sizes)
        here = linear_place(axes, sizes)
        width = inputs[i].shape[-1]
        own = pltpu.make_async_copy(
            part(kind, inputs[i], here, size),
            landing(kind, outputs[i], here, width),
            sems[3 * i + 2].at[0],
        )
        own.start()
        local_copies.append(own)
    pl.semaphore_wait(barrier, total)
    copies = []
    for i, (kind, axes) in enumerate(kinds):
        size = count(axes, sizes)
        here = linear_place(axes, sizes)
        width = inputs[i].shape[-1]
        for k in range(1, size):
            place = lax.rem(here + k, size)
            copy = pltpu.make_async_remote_copy(
                src_ref=part(kind, inputs[i], place, size),
                dst_ref=landing(kind, outputs[i], here, width),
                send_sem=sems[3 * i].at[k - 1],
                recv_sem=sems[3 * i + 1].at[k - 1],
                device_id=coordinates(axes, sizes, place),
                device_id_type=MESH,
            )
            copy.start()
            copies.append(copy)
    for own in local_copies:
        own.wait()
    for copy in copies:
        copy.wait()


def exchange(sizes, number, *items):
    kinds = tuple((kind, axes) for _, kind, axes in items)
    shapes, scratch = [], []
    for array, kind, axes in items:
        size = count(axes, sizes)
        if kind == "gather":
            shape = (size,) + array.shape
        elif kind == "rows":
            shape = array.shape
        elif kind == "second":
            shape = (size, array.shape[0]) + array.shape[2:]
        elif kind == "columns":
            shape = (size, array.shape[0], array.shape[1] // size)
        else:
            shape = (array.shape[1], size * array.shape[2])
        shapes.append(jax.ShapeDtypeStruct(shape, array.dtype))
        scratch += [
            pltpu.SemaphoreType.DMA((size - 1,)),
            pltpu.SemaphoreType.DMA((size - 1,)),
            pltpu.SemaphoreType.DMA((1,)),
        ]
    return pl.pallas_call(
        functools.partial(exchange_kernel, kinds, sizes),
        out_shape=tuple(shapes),
        in_specs=[pl.BlockSpec(memory_space=pl.ANY)] * len(items),
        out_specs=tuple(pl.BlockSpec(memory_space=pl.ANY) for _ in items),
        scratch_shapes=scratch,
        compiler_params=pltpu.CompilerParams(collective_id=number, has_side_effects=True),
        name=f"exchange_{number}",
    )(*(array for array, _, _ in items))


def greet(sizes):
    d, f, e = lax.axis_index("dp"), lax.axis_index("fsdp"), lax.axis_index("expert")
    levels = sizes["expert"] // 2
    y, c = e // 2, lax.rem(e, 2)
    barrier = pltpu.get_barrier_semaphore()
    others = []
    for k in range(1, sizes["dp"]):
        others.append({"dp": lax.rem(d + k, sizes["dp"])})
    for k in range(1, sizes["fsdp"]):
        others.append({"fsdp": lax.rem(f + k, sizes["fsdp"])})
    for k in range(1, levels):
        others.append({"expert": lax.rem(y + k, levels) * 2 + c})
    others.append({"expert": y * 2 + 1 - c})
    for other in others:
        pl.semaphore_signal(barrier, inc=1, device_id=other, device_id_type=MESH)
    pl.semaphore_wait(barrier, len(others))
    return d, f, e, y, c


class Sender:
    def __init__(self, send, recv):
        self.send, self.recv, self.next = send, recv, 0

    def __call__(self, source, target, device):
        copy = pltpu.make_async_remote_copy(
            src_ref=source,
            dst_ref=target,
            send_sem=self.send.at[self.next],
            recv_sem=self.recv.at[self.next],
            device_id=device,
            device_id_type=MESH,
        )
        self.next += 1
        copy.start()
        return copy


def spread_kernel(sizes, x_ref, g_ref, out, gates, send, recv, local):
    dps, fs, levels = sizes["dp"], sizes["fsdp"], sizes["expert"] // 2
    own = [
        pltpu.make_async_copy(
            x_ref,
            out.at[
                lax.axis_index("dp"),
                lax.axis_index("fsdp"),
                lax.axis_index("expert") // 2,
                lax.rem(lax.axis_index("expert"), 2),
            ],
            local.at[0],
        ),
        pltpu.make_async_copy(
            g_ref,
            gates.at[
                lax.axis_index("dp"),
                lax.axis_index("fsdp"),
                lax.axis_index("expert") // 2,
                lax.rem(lax.axis_index("expert"), 2),
            ],
            local.at[1],
        ),
    ]
    for copy in own:
        copy.start()
    d, f, e, y, c = greet(sizes)
    half = x_ref.shape[-1] // 2
    low, high = pl.ds(0, half), pl.ds(half, half)
    go = Sender(send, recv)
    copies = []
    for k in range(1, fs):
        to = {"fsdp": lax.rem(f + k, fs)}
        copies.append(go(x_ref, out.at[d, f, y, c], to))
        copies.append(go(g_ref, gates.at[d, f, y, c], to))
    for copy in own:
        copy.wait()
    for copy in copies:
        copy.wait()
    copies = []
    for k in range(1, dps):
        to = {"dp": lax.rem(d + k, dps)}
        part = out.at[d, :, y, c, :, low]
        copies.append(go(part, part, to))
        part = gates.at[d, :, y, c]
        copies.append(go(part, part, to))
    for k in range(1, levels):
        to = {"expert": lax.rem(y + k, levels) * 2 + c}
        part = out.at[d, :, y, c, :, high]
        copies.append(go(part, part, to))
    for copy in copies:
        copy.wait()
    copies = []
    for k in range(1, levels):
        to = {"expert": lax.rem(y + k, levels) * 2 + c}
        part = out.at[:, :, y, c, :, low]
        copies.append(go(part, part, to))
        part = gates.at[:, :, y, c]
        copies.append(go(part, part, to))
    for k in range(1, dps):
        to = {"dp": lax.rem(d + k, dps)}
        part = out.at[d, :, :, c, :, high]
        copies.append(go(part, part, to))
    for copy in copies:
        copy.wait()
    to = {"expert": y * 2 + 1 - c}
    part = out.at[:, :, :, c]
    copies = [go(part, part, to)]
    part = gates.at[:, :, :, c]
    copies.append(go(part, part, to))
    for copy in copies:
        copy.wait()


def spread(sizes, number, rows, shares):
    dps, fs, levels = sizes["dp"], sizes["fsdp"], sizes["expert"] // 2
    lead = (dps, fs, levels, 2)
    sems = 2 * (fs - 1) + 3 * (dps - 1) + 3 * (levels - 1) + 2
    return pl.pallas_call(
        functools.partial(spread_kernel, sizes),
        out_shape=(
            jax.ShapeDtypeStruct(lead + rows.shape, rows.dtype),
            jax.ShapeDtypeStruct(lead + shares.shape, shares.dtype),
        ),
        in_specs=[pl.BlockSpec(memory_space=pl.ANY)] * 2,
        out_specs=(pl.BlockSpec(memory_space=pl.ANY),) * 2,
        scratch_shapes=[
            pltpu.SemaphoreType.DMA((sems,)),
            pltpu.SemaphoreType.DMA((sems,)),
            pltpu.SemaphoreType.DMA((2,)),
        ],
        compiler_params=pltpu.CompilerParams(collective_id=number, has_side_effects=True),
        name="spread",
    )(rows, shares)


def collect_kernel(
    sizes, x_ref, out, first, one, two_a, two_b, three, r1, r2a, r2b, r3a, r3b, r4, send, recv, local
):
    dps, fs, levels = sizes["dp"], sizes["fsdp"], sizes["expert"] // 2
    half = out.shape[-1] // 2
    low, high = pl.ds(0, half), pl.ds(half, half)
    own = pltpu.make_async_copy(
        x_ref.at[:, :, :, lax.rem(lax.axis_index("expert"), 2)], first, local.at[0]
    )
    own.start()
    d, f, e, y, c = greet(sizes)
    go = Sender(send, recv)
    copy = go(x_ref.at[:, :, :, 1 - c], r1, {"expert": y * 2 + 1 - c})
    own.wait()
    copy.wait()

    @pl.loop(0, dps * fs * levels)
    def _(i):
        p, q, r = i // (fs * levels), lax.rem(i // levels, fs), lax.rem(i, levels)
        one[p, q, r] = (
            first[p, q, r].astype(jnp.float32) + r1[p, q, r].astype(jnp.float32)
        ).astype(one.dtype)

    copies = []
    for k in range(1, dps):
        to = lax.rem(d + k, dps)
        copies.append(go(one.at[to, :, :, :, low], r2a.at[k - 1], {"dp": to}))
    for k in range(1, levels):
        to = lax.rem(y + k, levels)
        copies.append(go(one.at[:, :, to, :, high], r2b.at[k - 1], {"expert": to * 2 + c}))
    for copy in copies:
        copy.wait()

    @pl.loop(0, fs * levels)
    def _(i):
        q, r = i // levels, lax.rem(i, levels)
        total = one[d, q, r, :, low].astype(jnp.float32)
        for k in range(dps - 1):
            total += r2a[k, q, r].astype(jnp.float32)
        two_a[q, r] = total.astype(two_a.dtype)

    @pl.loop(0, dps * fs)
    def _(i):
        p, q = i // fs, lax.rem(i, fs)
        total = one[p, q, y, :, high].astype(jnp.float32)
        for k in range(levels - 1):
            total += r2b[k, p, q].astype(jnp.float32)
        two_b[p, q] = total.astype(two_b.dtype)

    copies = []
    for k in range(1, levels):
        to = lax.rem(y + k, levels)
        copies.append(go(two_a.at[:, to], r3a.at[k - 1], {"expert": to * 2 + c}))
    for k in range(1, dps):
        to = lax.rem(d + k, dps)
        copies.append(go(two_b.at[to], r3b.at[k - 1], {"dp": to}))
    for copy in copies:
        copy.wait()

    @pl.loop(0, fs)
    def _(q):
        total = two_a[q, y].astype(jnp.float32)
        for k in range(levels - 1):
            total += r3a[k, q].astype(jnp.float32)
        three[q, :, low] = total.astype(three.dtype)
        total = two_b[d, q].astype(jnp.float32)
        for k in range(dps - 1):
            total += r3b[k, q].astype(jnp.float32)
        three[q, :, high] = total.astype(three.dtype)

    copies = []
    for k in range(1, fs):
        to = lax.rem(f + k, fs)
        copies.append(go(three.at[to], r4.at[k - 1], {"fsdp": to}))
    for copy in copies:
        copy.wait()
    total = three[f].astype(jnp.float32)
    for k in range(fs - 1):
        total += r4[k].astype(jnp.float32)
    out[...] = total


def collect(sizes, number, terms):
    dps, fs, levels = sizes["dp"], sizes["fsdp"], sizes["expert"] // 2
    rows, width = terms.shape[-2:]
    half = width // 2
    kind = terms.dtype
    sems = 1 + 2 * (dps - 1) + 2 * (levels - 1) + (fs - 1)
    return pl.pallas_call(
        functools.partial(collect_kernel, sizes),
        out_shape=jax.ShapeDtypeStruct((rows, width), jnp.float32),
        in_specs=[pl.BlockSpec(memory_space=pl.ANY)],
        out_specs=pl.BlockSpec(memory_space=pltpu.VMEM),
        scratch_shapes=[
            pltpu.VMEM((dps, fs, levels, rows, width), kind),
            pltpu.VMEM((dps, fs, levels, rows, width), kind),
            pltpu.VMEM((fs, levels, rows, half), kind),
            pltpu.VMEM((dps, fs, rows, half), kind),
            pltpu.VMEM((fs, rows, width), kind),
            pltpu.VMEM((dps, fs, levels, rows, width), kind),
            pltpu.VMEM((dps - 1, fs, levels, rows, half), kind),
            pltpu.VMEM((levels - 1, dps, fs, rows, half), kind),
            pltpu.VMEM((levels - 1, fs, rows, half), kind),
            pltpu.VMEM((dps - 1, fs, rows, half), kind),
            pltpu.VMEM((fs - 1, rows, width), kind),
            pltpu.SemaphoreType.DMA((sems,)),
            pltpu.SemaphoreType.DMA((sems,)),
            pltpu.SemaphoreType.DMA((1,)),
        ],
        compiler_params=pltpu.CompilerParams(
            collective_id=number, has_side_effects=True, vmem_limit_bytes=56 << 20
        ),
        name="collect",
    )(terms)


def local(
    sizes,
    window,
    attention_gain,
    query_weight,
    key_weight,
    value_weight,
    out_weight,
    cache_keys,
    cache_values,
    occluded,
    feedforward_gain,
    router_weight,
    chosen_experts,
    gate_weight,
    up_weight,
    down_weight,
):
    dps, fs, es = sizes["dp"], sizes["fsdp"], sizes["expert"]
    token_rows, width = window.shape
    d, f, e = lax.axis_index("dp"), lax.axis_index("fsdp"), lax.axis_index("expert")
    query_width = query_weight.shape[1]
    key_width = key_weight.shape[1]
    query_heads = query_width // HD
    key_heads = key_width // HD
    grouping = query_heads // key_heads
    window_rows = token_rows * fs
    prefix_rows = cache_keys.shape[0] * dps
    score_scale = HD ** (-0.5)
    part = token_rows // dps
    sub = token_rows // es

    own_rows = lax.dynamic_slice_in_dim(window, d * part, part, 0)
    normed = rms_norm(own_rows, attention_gain)
    flags = occluded.astype(jnp.float32).T
    columns, keys_block, values_block, flags_block = exchange(
        sizes,
        0,
        (normed, "columns", ("fsdp",)),
        (cache_keys, "gather", ("dp",)),
        (cache_values, "gather", ("dp",)),
        (flags, "gather", ("dp",)),
    )
    columns = columns.reshape(fs * part, width // fs)
    sums = jnp.concatenate(
        [
            jnp.dot(columns, weight, preferred_element_type=jnp.float32)
            for weight in (query_weight, key_weight, value_weight)
        ],
        axis=1,
    )
    (sums,) = exchange(sizes, 1, (sums.reshape(fs, part, -1), "rows", ("fsdp",)))
    sums = jnp.sum(sums, axis=0)
    positions = prefix_rows + f * token_rows + d * part + jnp.arange(part, dtype=jnp.int32)
    rotated = rotate(
        sums[:, : query_width + key_width].reshape(part, query_heads + key_heads, HD), positions
    ).astype(jnp.bfloat16)
    queries = rotated[:, :query_heads].reshape(part, query_width)
    fresh = jnp.concatenate(
        [
            rotated[:, query_heads:].reshape(part, key_width),
            sums[:, query_width + key_width :].astype(jnp.bfloat16),
        ],
        axis=1,
    )
    queries, fresh = exchange(
        sizes, 2, (queries, "gather", ("dp",)), (fresh, "gather", ("fsdp", "dp"))
    )
    fresh = fresh.reshape(window_rows, 2 * key_width)
    query_grid = queries.reshape(token_rows, key_heads, grouping, HD)
    all_keys = jnp.concatenate(
        [keys_block.reshape(prefix_rows, key_width), fresh[:, :key_width]], axis=0
    ).reshape(prefix_rows + window_rows, key_heads, HD)
    all_values = jnp.concatenate(
        [values_block.reshape(prefix_rows, key_width), fresh[:, key_width:]], axis=0
    ).reshape(prefix_rows + window_rows, key_heads, HD)
    scores = (
        jnp.einsum("tkgd,nkd->kgtn", query_grid, all_keys, preferred_element_type=jnp.float32)
        * score_scale
    )
    seen = lax.dynamic_slice_in_dim(flags_block, d, 1, 1).reshape(prefix_rows) == 0
    causal = (
        jnp.arange(window_rows)[None, :]
        <= (f * token_rows + jnp.arange(token_rows))[:, None]
    )
    visible = jnp.concatenate(
        [jnp.broadcast_to(seen[None, :], (token_rows, prefix_rows)), causal], axis=1
    )
    masked = jnp.where(visible, scores, floor_score)
    top = jnp.max(masked, axis=-1, keepdims=True)
    weights = jnp.exp(masked - top)
    totals = jnp.sum(weights, axis=-1)
    heads = jnp.einsum(
        "kgtn,nkd->tkgd",
        weights.astype(jnp.bfloat16),
        all_values,
        preferred_element_type=jnp.float32,
    ) / totals.transpose(2, 0, 1)[..., None]
    attended = heads.reshape(token_rows, query_width).astype(jnp.bfloat16)

    (attended,) = exchange(sizes, 3, (attended, "gather", ("fsdp",)))
    head_terms = jnp.dot(
        attended.reshape(window_rows, query_width), out_weight, preferred_element_type=jnp.float32
    )
    (head_terms,) = exchange(
        sizes, 4, (head_terms.reshape(fs, es, sub, -1), "second", ("expert",))
    )
    (projected,) = exchange(
        sizes, 5, (jnp.sum(head_terms, axis=0), "rows_to_columns", ("fsdp",))
    )
    residual = lax.dynamic_slice_in_dim(window, e * sub, sub, 0).astype(jnp.float32) + projected
    normed_mix = rms_norm(residual, feedforward_gain)
    logits = jnp.dot(normed_mix, router_weight, preferred_element_type=jnp.float32)
    picks = lax.dynamic_slice_in_dim(chosen_experts.reshape(token_rows, TOP), e * sub, sub, 0)
    experts = router_weight.shape[1]
    matches = picks[:, :, None] == jnp.arange(experts, dtype=jnp.int32)[None, None, :]
    picked = jnp.sum(jnp.where(matches, logits[:, None, :], 0.0), axis=-1)
    gate_shares = jax.nn.sigmoid(picked - picked[:, ::-1])
    lanes = picks[:, :, None] == jnp.arange(128, dtype=jnp.int32)[None, None, :]
    shares = jnp.sum(jnp.where(lanes, gate_shares[:, :, None], 0.0), axis=1)

    rows, shares = spread(sizes, 6, normed_mix, shares)
    every = dps * window_rows
    rows = rows.reshape(every, width)
    share = lax.dynamic_slice_in_dim(shares.reshape(every, 128), e, 1, 1)
    contract_last = (((1,), (1,)), ((), ()))
    gate_values = lax.dot_general(
        rows, gate_weight[0], contract_last, preferred_element_type=jnp.float32
    )
    lifted = lax.dot_general(rows, up_weight[0], contract_last, preferred_element_type=jnp.float32)
    hidden = (jax.nn.silu(gate_values) * lifted).astype(jnp.bfloat16)
    terms = (
        jnp.dot(hidden, down_weight[0], preferred_element_type=jnp.float32) * share
    ).astype(jnp.bfloat16)
    mixture = collect(sizes, 7, terms.reshape(dps, fs, es // 2, 2, sub, width))
    (whole,) = exchange(
        sizes, 8, ((residual + mixture).astype(jnp.bfloat16), "gather", ("expert",))
    )
    return whole.reshape(1, token_rows, width)


def solution(mesh):
    sizes = dict(mesh.shape)
    placed = (
        P("fsdp", None),
        P(),
        P("fsdp", "expert"),
        P("fsdp", "expert"),
        P("fsdp", "expert"),
        P("expert", "fsdp"),
        P("dp", "expert"),
        P("dp", "expert"),
        P("dp", None),
        P(),
        P(),
        P("dp", "fsdp", None),
        P("expert", ("dp", "fsdp"), None),
        P("expert", ("dp", "fsdp"), None),
        P("expert", ("dp", "fsdp"), None),
    )
    return jax.shard_map(
        functools.partial(local, sizes),
        mesh=mesh,
        in_specs=placed,
        out_specs=P("dp", "fsdp", None),
        check_vma=False,
    )
```

```python
import functools

import jax
import jax.numpy as jnp
from jax import lax
from jax.experimental import pallas as pl
from jax.experimental.pallas import tpu as pltpu
from jax.sharding import PartitionSpec as P

HD = 128
TOP = 2

epsilon = 1e-05
rope_base = 1000000.0
floor_score = -1e30
MESH = pl.DeviceIdType.MESH


def rms_norm(values, scales):
    widened = values.astype(jnp.float32)
    inverse = lax.rsqrt(jnp.mean(widened * widened, axis=-1, keepdims=True) + epsilon)
    return (widened * inverse * scales).astype(jnp.bfloat16)


def rotate(vectors, positions):
    halfway = vectors.shape[-1] // 2
    powers = jnp.arange(halfway, dtype=jnp.float32) * (2.0 / vectors.shape[-1])
    frequency = rope_base ** (-powers)
    angles = positions.astype(jnp.float32)[:, None] * frequency[None, :]
    cosine = jnp.cos(angles)[:, None, :]
    sine_part = jnp.sin(angles)[:, None, :]
    former = vectors[..., :halfway]
    latter = vectors[..., halfway:]
    return jnp.concatenate(
        [former * cosine - latter * sine_part, latter * cosine + former * sine_part], axis=-1
    )


def linear_place(axes, sizes):
    place = 0
    for axis in axes:
        place = place * sizes[axis] + lax.axis_index(axis)
    return place


def coordinates(axes, sizes, place):
    found = {}
    for axis in reversed(axes):
        found[axis] = lax.rem(place, sizes[axis])
        place = place // sizes[axis]
    return found


def count(axes, sizes):
    total = 1
    for axis in axes:
        total *= sizes[axis]
    return total


def source_part(kind, ref, to):
    if kind == "gather":
        return ref
    if kind == "rows":
        return ref.at[to]
    if kind == "second":
        return ref.at[:, to]
    if kind == "rows_to_columns":
        return ref.at[to]
    raise ValueError(kind)


def exchange_kernel(kinds, sizes, *refs):
    n = len(kinds)
    inputs, outputs, sems = refs[:n], refs[n : 2 * n], refs[2 * n :]
    barrier = pltpu.get_barrier_semaphore()
    total = 0
    for _, axes in kinds:
        size = count(axes, sizes)
        here = linear_place(axes, sizes)
        for k in range(1, size):
            to = coordinates(axes, sizes, lax.rem(here + k, size))
            pl.semaphore_signal(barrier, inc=1, device_id=to, device_id_type=MESH)
        total += size - 1
    local_copies = []

    def landing(kind, out, here, width):
        if kind == "rows_to_columns":
            return out.at[:, pl.ds(pl.multiple_of(here * width, 128), width)]
        return out.at[here]

    def part(kind, ref, to, size):
        if kind == "columns":
            width = ref.shape[1] // size
            return ref.at[:, pl.ds(pl.multiple_of(to * width, 128), width)]
        return source_part(kind, ref, to)

    for i, (kind, axes) in enumerate(kinds):
        size = count(axes, sizes)
        here = linear_place(axes, sizes)
        width = inputs[i].shape[-1]
        own = pltpu.make_async_copy(
            part(kind, inputs[i], here, size),
            landing(kind, outputs[i], here, width),
            sems[3 * i + 2].at[0],
        )
        own.start()
        local_copies.append(own)
    pl.semaphore_wait(barrier, total)
    copies = []
    for i, (kind, axes) in enumerate(kinds):
        size = count(axes, sizes)
        here = linear_place(axes, sizes)
        width = inputs[i].shape[-1]
        for k in range(1, size):
            place = lax.rem(here + k, size)
            copy = pltpu.make_async_remote_copy(
                src_ref=part(kind, inputs[i], place, size),
                dst_ref=landing(kind, outputs[i], here, width),
                send_sem=sems[3 * i].at[k - 1],
                recv_sem=sems[3 * i + 1].at[k - 1],
                device_id=coordinates(axes, sizes, place),
                device_id_type=MESH,
            )
            copy.start()
            copies.append(copy)
    for own in local_copies:
        own.wait()
    for copy in copies:
        copy.wait()


def exchange(sizes, number, *items):
    kinds = tuple((kind, axes) for _, kind, axes in items)
    shapes, scratch = [], []
    for array, kind, axes in items:
        size = count(axes, sizes)
        if kind == "gather":
            shape = (size,) + array.shape
        elif kind == "rows":
            shape = array.shape
        elif kind == "second":
            shape = (size, array.shape[0]) + array.shape[2:]
        elif kind == "columns":
            shape = (size, array.shape[0], array.shape[1] // size)
        else:
            shape = (array.shape[1], size * array.shape[2])
        shapes.append(jax.ShapeDtypeStruct(shape, array.dtype))
        scratch += [
            pltpu.SemaphoreType.DMA((size - 1,)),
            pltpu.SemaphoreType.DMA((size - 1,)),
            pltpu.SemaphoreType.DMA((1,)),
        ]
    return pl.pallas_call(
        functools.partial(exchange_kernel, kinds, sizes),
        out_shape=tuple(shapes),
        in_specs=[pl.BlockSpec(memory_space=pl.ANY)] * len(items),
        out_specs=tuple(pl.BlockSpec(memory_space=pl.ANY) for _ in items),
        scratch_shapes=scratch,
        compiler_params=pltpu.CompilerParams(collective_id=number, has_side_effects=True),
        name=f"exchange_{number}",
    )(*(array for array, _, _ in items))


def greet(sizes):
    d, f, e = lax.axis_index("dp"), lax.axis_index("fsdp"), lax.axis_index("expert")
    levels = sizes["expert"] // 2
    y, c = e // 2, lax.rem(e, 2)
    barrier = pltpu.get_barrier_semaphore()
    others = []
    for k in range(1, sizes["dp"]):
        others.append({"dp": lax.rem(d + k, sizes["dp"])})
    for k in range(1, sizes["fsdp"]):
        others.append({"fsdp": lax.rem(f + k, sizes["fsdp"])})
    for k in range(1, levels):
        others.append({"expert": lax.rem(y + k, levels) * 2 + c})
    others.append({"expert": y * 2 + 1 - c})
    for other in others:
        pl.semaphore_signal(barrier, inc=1, device_id=other, device_id_type=MESH)
    pl.semaphore_wait(barrier, len(others))
    return d, f, e, y, c


class Sender:
    def __init__(self, send, recv):
        self.send, self.recv, self.next = send, recv, 0

    def __call__(self, source, target, device):
        copy = pltpu.make_async_remote_copy(
            src_ref=source,
            dst_ref=target,
            send_sem=self.send.at[self.next],
            recv_sem=self.recv.at[self.next],
            device_id=device,
            device_id_type=MESH,
        )
        self.next += 1
        copy.start()
        return copy


def flat_rows(block, rows):
    if block.shape[-2] % 16 == 0:
        return block.reshape(rows, block.shape[-1])
    return block.astype(jnp.float32).reshape(rows, block.shape[-1]).astype(block.dtype)


def open_rows(block, lead):
    if lead[-1] % 16 == 0:
        return block.astype(jnp.bfloat16).reshape(lead + block.shape[-1:])
    return block.reshape(lead + block.shape[-1:]).astype(jnp.bfloat16)


def spread_kernel(
    sizes, pieces, x_ref, g_ref, gate_ref, up_ref, hidden, gates,
    rows, gate_w, up_w, gate_sum, up_sum, send, recv, local, weight_sems,
):
    dps, fs, levels = sizes["dp"], sizes["fsdp"], sizes["expert"] // 2
    place = (
        lax.axis_index("dp"),
        lax.axis_index("fsdp"),
        lax.axis_index("expert") // 2,
        lax.rem(lax.axis_index("expert"), 2),
    )
    own = [
        pltpu.make_async_copy(x_ref, rows.at[place], local.at[0]),
        pltpu.make_async_copy(g_ref, gates.at[place], local.at[1]),
    ]
    for copy in own:
        copy.start()
    wide = x_ref.shape[-1] // pieces
    half = wide // 2
    loads = []
    for j in range(pieces):
        cols = pl.ds(j * wide, wide)
        pair = [
            pltpu.make_async_copy(gate_ref.at[0, :, cols], gate_w.at[:, cols], weight_sems.at[2 * j]),
            pltpu.make_async_copy(up_ref.at[0, :, cols], up_w.at[:, cols], weight_sems.at[2 * j + 1]),
        ]
        loads.append(pair)
    d, f, e, y, c = greet(sizes)
    go = Sender(send, recv)
    flying = {}

    def start(phase, j):
        low, high = pl.ds(j * wide, half), pl.ds(j * wide + half, half)
        full = pl.ds(j * wide, wide)
        copies = []
        if phase == 0:
            for k in range(1, fs):
                to = {"fsdp": lax.rem(f + k, fs)}
                copies.append(go(x_ref.at[:, full], rows.at[d, f, y, c, :, full], to))
                if j == 0:
                    copies.append(go(g_ref, gates.at[d, f, y, c], to))
        elif phase == 1:
            for k in range(1, dps):
                to = {"dp": lax.rem(d + k, dps)}
                block = rows.at[d, :, y, c, :, low]
                copies.append(go(block, block, to))
                if j == 0:
                    block = gates.at[d, :, y, c]
                    copies.append(go(block, block, to))
            for k in range(1, levels):
                to = {"expert": lax.rem(y + k, levels) * 2 + c}
                block = rows.at[d, :, y, c, :, high]
                copies.append(go(block, block, to))
        elif phase == 2:
            for k in range(1, levels):
                to = {"expert": lax.rem(y + k, levels) * 2 + c}
                block = rows.at[:, :, y, c, :, low]
                copies.append(go(block, block, to))
                if j == 0:
                    block = gates.at[:, :, y, c]
                    copies.append(go(block, block, to))
            for k in range(1, dps):
                to = {"dp": lax.rem(d + k, dps)}
                block = rows.at[d, :, :, c, :, high]
                copies.append(go(block, block, to))
        else:
            to = {"expert": y * 2 + 1 - c}
            block = rows.at[:, :, :, c, :, full]
            copies.append(go(block, block, to))
            if j == 0:
                block = gates.at[:, :, :, c]
                copies.append(go(block, block, to))
        flying[phase, j] = copies

    def finish(phase, j):
        for copy in flying.pop((phase, j)):
            copy.wait()

    for j in range(pieces):
        start(0, j)
    for pair in loads:
        for copy in pair:
            copy.start()
    for copy in own:
        copy.wait()
    every, units = hidden.shape
    tile = 256 if units % 256 == 0 else 128
    for step in range(pieces + 3):
        for phase in (3, 2, 1):
            j = step - phase + 1
            if 0 <= j < pieces:
                finish(phase - 1, j)
                start(phase, j)
        j = step - 3
        if j < 0:
            continue
        finish(3, j)
        for copy in loads[j]:
            copy.wait()

        @pl.loop(0, units // tile)
        def _(i, j=j):
            full = pl.ds(j * wide, wide)
            picked = pl.ds(pl.multiple_of(i * tile, tile), tile)
            block = flat_rows(rows[:, :, :, :, :, full], every)
            last = (((1,), (1,)), ((), ()))
            g = lax.dot_general(
                block, gate_w[picked, full], last, preferred_element_type=jnp.float32
            )
            u = lax.dot_general(block, up_w[picked, full], last, preferred_element_type=jnp.float32)
            if j > 0:
                g += gate_sum[:, picked]
                u += up_sum[:, picked]
            if j < pieces - 1:
                gate_sum[:, picked] = g
                up_sum[:, picked] = u
            else:
                hidden[:, picked] = (g / (1.0 + jnp.exp(-g)) * u).astype(hidden.dtype)


def spread(sizes, number, rows, shares, gate_weight, up_weight, pieces=4):
    dps, fs, levels = sizes["dp"], sizes["fsdp"], sizes["expert"] // 2
    lead = (dps, fs, levels, 2)
    sub, width = rows.shape
    every = dps * fs * levels * 2 * sub
    units = gate_weight.shape[1]
    gate_copies = (fs - 1) + (dps - 1) + (levels - 1) + 1
    sems = pieces * ((fs - 1) + 2 * (dps - 1) + 2 * (levels - 1) + 1) + gate_copies
    return pl.pallas_call(
        functools.partial(spread_kernel, sizes, pieces),
        out_shape=(
            jax.ShapeDtypeStruct((every, units), jnp.bfloat16),
            jax.ShapeDtypeStruct(lead + shares.shape, shares.dtype),
        ),
        in_specs=[pl.BlockSpec(memory_space=pl.ANY)] * 4,
        out_specs=(pl.BlockSpec(memory_space=pltpu.VMEM), pl.BlockSpec(memory_space=pl.ANY)),
        scratch_shapes=[
            pltpu.VMEM(lead + rows.shape, rows.dtype),
            pltpu.VMEM((units, width), rows.dtype),
            pltpu.VMEM((units, width), rows.dtype),
            pltpu.VMEM((every, units), jnp.float32),
            pltpu.VMEM((every, units), jnp.float32),
            pltpu.SemaphoreType.DMA((sems,)),
            pltpu.SemaphoreType.DMA((sems,)),
            pltpu.SemaphoreType.DMA((2,)),
            pltpu.SemaphoreType.DMA((2 * pieces,)),
        ],
        compiler_params=pltpu.CompilerParams(
            collective_id=number, has_side_effects=True, vmem_limit_bytes=56 << 20
        ),
        name="spread",
    )(rows, shares, gate_weight, up_weight)


def collect_kernel(
    sizes, pieces, hidden, share, down_ref, out,
    terms, down_w, one, two_a, two_b, three, r1, r2a, r2b, r3a, r3b, r4, send, recv, weight_sems,
):
    dps, fs, levels = sizes["dp"], sizes["fsdp"], sizes["expert"] // 2
    sub, width = out.shape
    wide = width // pieces
    half = wide // 2
    loads = []
    for j in range(pieces):
        cols = pl.ds(j * wide, wide)
        copy = pltpu.make_async_copy(down_ref.at[0, :, cols], down_w.at[:, cols], weight_sems.at[j])
        copy.start()
        loads.append(copy)
    d, f, e, y, c = greet(sizes)
    go = Sender(send, recv)
    flying = {}
    wider = jnp.float32
    tile = 256

    def finish(phase, j):
        for copy in flying.pop((phase, j)):
            copy.wait()

    def make(j):
        loads[j].wait()

        @pl.loop(0, wide // tile)
        def _(i):
            picked = pl.ds(pl.multiple_of(j * wide + i * tile, tile), tile)
            product = jnp.dot(hidden[...], down_w[:, picked], preferred_element_type=wider)
            terms[:, :, :, :, :, picked] = open_rows(
                product * share[...], (dps, fs, levels, 2, sub)
            )

        full = pl.ds(j * wide, wide)
        flying[0, j] = [
            go(terms.at[:, :, :, 1 - c, :, full], r1.at[:, :, :, :, full], {"expert": y * 2 + 1 - c})
        ]

    def after_chip(j):
        finish(0, j)
        low, high = pl.ds(j * wide, half), pl.ds(j * wide + half, half)
        full = pl.ds(j * wide, wide)
        narrow = pl.ds(j * half, half)

        @pl.loop(0, dps * fs * levels)
        def _(i):
            p, q, r = i // (fs * levels), lax.rem(i // levels, fs), lax.rem(i, levels)
            one[p, q, r, :, full] = (
                terms[p, q, r, c, :, full].astype(wider) + r1[p, q, r, :, full].astype(wider)
            ).astype(one.dtype)

        copies = []
        for k in range(1, dps):
            to = lax.rem(d + k, dps)
            copies.append(
                go(one.at[to, :, :, :, low], r2a.at[k - 1, :, :, :, narrow], {"dp": to})
            )
        for k in range(1, levels):
            to = lax.rem(y + k, levels)
            copies.append(
                go(one.at[:, :, to, :, high], r2b.at[k - 1, :, :, :, narrow], {"expert": to * 2 + c})
            )
        flying[1, j] = copies

    def after_first(j):
        finish(1, j)
        low, high = pl.ds(j * wide, half), pl.ds(j * wide + half, half)
        narrow = pl.ds(j * half, half)

        @pl.loop(0, fs * levels)
        def _(i):
            q, r = i // levels, lax.rem(i, levels)
            total = one[d, q, r, :, low].astype(wider)
            for k in range(dps - 1):
                total += r2a[k, q, r, :, narrow].astype(wider)
            two_a[q, r, :, narrow] = total.astype(two_a.dtype)

        @pl.loop(0, dps * fs)
        def _(i):
            p, q = i // fs, lax.rem(i, fs)
            total = one[p, q, y, :, high].astype(wider)
            for k in range(levels - 1):
                total += r2b[k, p, q, :, narrow].astype(wider)
            two_b[p, q, :, narrow] = total.astype(two_b.dtype)

        copies = []
        for k in range(1, levels):
            to = lax.rem(y + k, levels)
            copies.append(
                go(two_a.at[:, to, :, narrow], r3a.at[k - 1, :, :, narrow], {"expert": to * 2 + c})
            )
        for k in range(1, dps):
            to = lax.rem(d + k, dps)
            copies.append(go(two_b.at[to, :, :, narrow], r3b.at[k - 1, :, :, narrow], {"dp": to}))
        flying[2, j] = copies

    def after_second(j):
        finish(2, j)
        low, high = pl.ds(j * wide, half), pl.ds(j * wide + half, half)
        full = pl.ds(j * wide, wide)
        narrow = pl.ds(j * half, half)

        @pl.loop(0, fs)
        def _(q):
            total = two_a[q, y, :, narrow].astype(wider)
            for k in range(levels - 1):
                total += r3a[k, q, :, narrow].astype(wider)
            three[q, :, low] = total.astype(three.dtype)
            total = two_b[d, q, :, narrow].astype(wider)
            for k in range(dps - 1):
                total += r3b[k, q, :, narrow].astype(wider)
            three[q, :, high] = total.astype(three.dtype)

        copies = []
        for k in range(1, fs):
            to = lax.rem(f + k, fs)
            copies.append(go(three.at[to, :, full], r4.at[k - 1, :, full], {"fsdp": to}))
        flying[3, j] = copies

    def after_third(j):
        finish(3, j)
        full = pl.ds(j * wide, wide)
        total = three[f, :, full].astype(wider)
        for k in range(fs - 1):
            total += r4[k, :, full].astype(wider)
        out[:, full] = total

    stages = (make, after_chip, after_first, after_second, after_third)
    for step in range(pieces + len(stages) - 1):
        for age, stage in enumerate(stages):
            if 0 <= step - age < pieces:
                stage(step - age)


def collect(sizes, number, hidden, share, down_weight, sub, pieces=4):
    dps, fs, levels = sizes["dp"], sizes["fsdp"], sizes["expert"] // 2
    units, width = down_weight.shape[1:]
    half = width // 2
    kind = jnp.bfloat16
    sems = pieces * (1 + 2 * (dps - 1) + 2 * (levels - 1) + (fs - 1))
    return pl.pallas_call(
        functools.partial(collect_kernel, sizes, pieces),
        out_shape=jax.ShapeDtypeStruct((sub, width), jnp.float32),
        in_specs=[
            pl.BlockSpec(memory_space=pltpu.VMEM),
            pl.BlockSpec(memory_space=pltpu.VMEM),
            pl.BlockSpec(memory_space=pl.ANY),
        ],
        out_specs=pl.BlockSpec(memory_space=pltpu.VMEM),
        scratch_shapes=[
            pltpu.VMEM((dps, fs, levels, 2, sub, width), kind),
            pltpu.VMEM((units, width), kind),
            pltpu.VMEM((dps, fs, levels, sub, width), kind),
            pltpu.VMEM((fs, levels, sub, half), kind),
            pltpu.VMEM((dps, fs, sub, half), kind),
            pltpu.VMEM((fs, sub, width), kind),
            pltpu.VMEM((dps, fs, levels, sub, width), kind),
            pltpu.VMEM((dps - 1, fs, levels, sub, half), kind),
            pltpu.VMEM((levels - 1, dps, fs, sub, half), kind),
            pltpu.VMEM((levels - 1, fs, sub, half), kind),
            pltpu.VMEM((dps - 1, fs, sub, half), kind),
            pltpu.VMEM((fs - 1, sub, width), kind),
            pltpu.SemaphoreType.DMA((sems,)),
            pltpu.SemaphoreType.DMA((sems,)),
            pltpu.SemaphoreType.DMA((pieces,)),
        ],
        compiler_params=pltpu.CompilerParams(
            collective_id=number, has_side_effects=True, vmem_limit_bytes=56 << 20
        ),
        name="collect",
    )(hidden, share, down_weight)


def local(
    sizes,
    window,
    attention_gain,
    query_weight,
    key_weight,
    value_weight,
    out_weight,
    cache_keys,
    cache_values,
    occluded,
    feedforward_gain,
    router_weight,
    chosen_experts,
    gate_weight,
    up_weight,
    down_weight,
):
    dps, fs, es = sizes["dp"], sizes["fsdp"], sizes["expert"]
    token_rows, width = window.shape
    d, f, e = lax.axis_index("dp"), lax.axis_index("fsdp"), lax.axis_index("expert")
    query_width = query_weight.shape[1]
    key_width = key_weight.shape[1]
    query_heads = query_width // HD
    key_heads = key_width // HD
    grouping = query_heads // key_heads
    window_rows = token_rows * fs
    prefix_rows = cache_keys.shape[0] * dps
    score_scale = HD ** (-0.5)
    part = token_rows // dps
    sub = token_rows // es

    own_rows = lax.dynamic_slice_in_dim(window, d * part, part, 0)
    normed = rms_norm(own_rows, attention_gain)
    flags = occluded.astype(jnp.float32).T
    columns, keys_block, values_block, flags_block = exchange(
        sizes,
        0,
        (normed, "columns", ("fsdp",)),
        (cache_keys, "gather", ("dp",)),
        (cache_values, "gather", ("dp",)),
        (flags, "gather", ("dp",)),
    )
    columns = columns.reshape(fs * part, width // fs)
    sums = jnp.concatenate(
        [
            jnp.dot(columns, weight, preferred_element_type=jnp.float32)
            for weight in (query_weight, key_weight, value_weight)
        ],
        axis=1,
    )
    (sums,) = exchange(sizes, 1, (sums.reshape(fs, part, -1), "rows", ("fsdp",)))
    sums = jnp.sum(sums, axis=0)
    positions = prefix_rows + f * token_rows + d * part + jnp.arange(part, dtype=jnp.int32)
    rotated = rotate(
        sums[:, : query_width + key_width].reshape(part, query_heads + key_heads, HD), positions
    ).astype(jnp.bfloat16)
    queries = rotated[:, :query_heads].reshape(part, query_width)
    fresh = jnp.concatenate(
        [
            rotated[:, query_heads:].reshape(part, key_width),
            sums[:, query_width + key_width :].astype(jnp.bfloat16),
        ],
        axis=1,
    )
    queries, fresh = exchange(
        sizes, 2, (queries, "gather", ("dp",)), (fresh, "gather", ("fsdp", "dp"))
    )
    fresh = fresh.reshape(window_rows, 2 * key_width)
    query_grid = queries.reshape(token_rows, key_heads, grouping, HD)
    all_keys = jnp.concatenate(
        [keys_block.reshape(prefix_rows, key_width), fresh[:, :key_width]], axis=0
    ).reshape(prefix_rows + window_rows, key_heads, HD)
    all_values = jnp.concatenate(
        [values_block.reshape(prefix_rows, key_width), fresh[:, key_width:]], axis=0
    ).reshape(prefix_rows + window_rows, key_heads, HD)
    scores = (
        jnp.einsum("tkgd,nkd->kgtn", query_grid, all_keys, preferred_element_type=jnp.float32)
        * score_scale
    )
    seen = lax.dynamic_slice_in_dim(flags_block, d, 1, 1).reshape(prefix_rows) == 0
    causal = (
        jnp.arange(window_rows)[None, :]
        <= (f * token_rows + jnp.arange(token_rows))[:, None]
    )
    visible = jnp.concatenate(
        [jnp.broadcast_to(seen[None, :], (token_rows, prefix_rows)), causal], axis=1
    )
    masked = jnp.where(visible, scores, floor_score)
    top = jnp.max(masked, axis=-1, keepdims=True)
    weights = jnp.exp(masked - top)
    totals = jnp.sum(weights, axis=-1)
    heads = jnp.einsum(
        "kgtn,nkd->tkgd",
        weights.astype(jnp.bfloat16),
        all_values,
        preferred_element_type=jnp.float32,
    ) / totals.transpose(2, 0, 1)[..., None]
    attended = heads.reshape(token_rows, query_width).astype(jnp.bfloat16)

    (attended,) = exchange(sizes, 3, (attended, "gather", ("fsdp",)))
    head_terms = jnp.dot(
        attended.reshape(window_rows, query_width), out_weight, preferred_element_type=jnp.float32
    )
    (head_terms,) = exchange(
        sizes, 4, (head_terms.reshape(fs, es, sub, -1), "second", ("expert",))
    )
    (projected,) = exchange(
        sizes, 5, (jnp.sum(head_terms, axis=0), "rows_to_columns", ("fsdp",))
    )
    residual = lax.dynamic_slice_in_dim(window, e * sub, sub, 0).astype(jnp.float32) + projected
    normed_mix = rms_norm(residual, feedforward_gain)
    logits = jnp.dot(normed_mix, router_weight, preferred_element_type=jnp.float32)
    picks = lax.dynamic_slice_in_dim(chosen_experts.reshape(token_rows, TOP), e * sub, sub, 0)
    experts = router_weight.shape[1]
    matches = picks[:, :, None] == jnp.arange(experts, dtype=jnp.int32)[None, None, :]
    picked = jnp.sum(jnp.where(matches, logits[:, None, :], 0.0), axis=-1)
    gate_shares = jax.nn.sigmoid(picked - picked[:, ::-1])
    lanes = picks[:, :, None] == jnp.arange(128, dtype=jnp.int32)[None, None, :]
    shares = jnp.sum(jnp.where(lanes, gate_shares[:, :, None], 0.0), axis=1)

    hidden, shares = spread(sizes, 6, normed_mix, shares, gate_weight, up_weight)
    share = lax.dynamic_slice_in_dim(shares.reshape(dps * window_rows, 128), e, 1, 1)
    mixture = collect(sizes, 7, hidden, share, down_weight, sub)
    (whole,) = exchange(
        sizes, 8, ((residual + mixture).astype(jnp.bfloat16), "gather", ("expert",))
    )
    return whole.reshape(1, token_rows, width)


def solution(mesh):
    sizes = dict(mesh.shape)
    placed = (
        P("fsdp", None),
        P(),
        P("fsdp", "expert"),
        P("fsdp", "expert"),
        P("fsdp", "expert"),
        P("expert", "fsdp"),
        P("dp", "expert"),
        P("dp", "expert"),
        P("dp", None),
        P(),
        P(),
        P("dp", "fsdp", None),
        P("expert", ("dp", "fsdp"), None),
        P("expert", ("dp", "fsdp"), None),
        P("expert", ("dp", "fsdp"), None),
    )
    return jax.shard_map(
        functools.partial(local, sizes),
        mesh=mesh,
        in_specs=placed,
        out_specs=P("dp", "fsdp", None),
        check_vma=False,
    )
```

```python
import functools

import jax
import jax.numpy as jnp
from jax import lax
from jax.experimental import pallas as pl
from jax.experimental.pallas import tpu as pltpu
from jax.sharding import PartitionSpec as P

HD = 128
TOP = 2

epsilon = 1e-05
rope_base = 1000000.0
floor_score = -1e30
MESH = pl.DeviceIdType.MESH


def rms_norm(values, scales):
    widened = values.astype(jnp.float32)
    inverse = lax.rsqrt(jnp.mean(widened * widened, axis=-1, keepdims=True) + epsilon)
    return (widened * inverse * scales).astype(jnp.bfloat16)


def rotate(vectors, positions):
    halfway = vectors.shape[-1] // 2
    powers = jnp.arange(halfway, dtype=jnp.float32) * (2.0 / vectors.shape[-1])
    frequency = rope_base ** (-powers)
    angles = positions.astype(jnp.float32)[:, None] * frequency[None, :]
    cosine = jnp.cos(angles)[:, None, :]
    sine_part = jnp.sin(angles)[:, None, :]
    former = vectors[..., :halfway]
    latter = vectors[..., halfway:]
    return jnp.concatenate(
        [former * cosine - latter * sine_part, latter * cosine + former * sine_part], axis=-1
    )


def linear_place(axes, sizes):
    place = 0
    for axis in axes:
        place = place * sizes[axis] + lax.axis_index(axis)
    return place


def coordinates(axes, sizes, place):
    found = {}
    for axis in reversed(axes):
        found[axis] = lax.rem(place, sizes[axis])
        place = place // sizes[axis]
    return found


def count(axes, sizes):
    total = 1
    for axis in axes:
        total *= sizes[axis]
    return total


def source_part(kind, ref, to):
    if kind == "gather":
        return ref
    if kind == "rows":
        return ref.at[to]
    if kind == "second":
        return ref.at[:, to]
    if kind == "rows_to_columns":
        return ref.at[to]
    raise ValueError(kind)


def exchange_kernel(kinds, sizes, *refs):
    n = len(kinds)
    inputs, outputs, sems = refs[:n], refs[n : 2 * n], refs[2 * n :]
    barrier = pltpu.get_barrier_semaphore()
    total = 0
    for _, axes in kinds:
        size = count(axes, sizes)
        here = linear_place(axes, sizes)
        for k in range(1, size):
            to = coordinates(axes, sizes, lax.rem(here + k, size))
            pl.semaphore_signal(barrier, inc=1, device_id=to, device_id_type=MESH)
        total += size - 1
    local_copies = []

    def landing(kind, out, here, width):
        if kind == "rows_to_columns":
            return out.at[:, pl.ds(pl.multiple_of(here * width, 128), width)]
        return out.at[here]

    def part(kind, ref, to, size):
        if kind == "columns":
            width = ref.shape[1] // size
            return ref.at[:, pl.ds(pl.multiple_of(to * width, 128), width)]
        return source_part(kind, ref, to)

    for i, (kind, axes) in enumerate(kinds):
        size = count(axes, sizes)
        here = linear_place(axes, sizes)
        width = inputs[i].shape[-1]
        own = pltpu.make_async_copy(
            part(kind, inputs[i], here, size),
            landing(kind, outputs[i], here, width),
            sems[3 * i + 2].at[0],
        )
        own.start()
        local_copies.append(own)
    pl.semaphore_wait(barrier, total)
    copies = []
    for i, (kind, axes) in enumerate(kinds):
        size = count(axes, sizes)
        here = linear_place(axes, sizes)
        width = inputs[i].shape[-1]
        for k in range(1, size):
            place = lax.rem(here + k, size)
            copy = pltpu.make_async_remote_copy(
                src_ref=part(kind, inputs[i], place, size),
                dst_ref=landing(kind, outputs[i], here, width),
                send_sem=sems[3 * i].at[k - 1],
                recv_sem=sems[3 * i + 1].at[k - 1],
                device_id=coordinates(axes, sizes, place),
                device_id_type=MESH,
            )
            copy.start()
            copies.append(copy)
    for own in local_copies:
        own.wait()
    for copy in copies:
        copy.wait()


def exchange(sizes, number, *items):
    kinds = tuple((kind, axes) for _, kind, axes in items)
    shapes, scratch = [], []
    for array, kind, axes in items:
        size = count(axes, sizes)
        if kind == "gather":
            shape = (size,) + array.shape
        elif kind == "rows":
            shape = array.shape
        elif kind == "second":
            shape = (size, array.shape[0]) + array.shape[2:]
        elif kind == "columns":
            shape = (size, array.shape[0], array.shape[1] // size)
        else:
            shape = (array.shape[1], size * array.shape[2])
        shapes.append(jax.ShapeDtypeStruct(shape, array.dtype))
        scratch += [
            pltpu.SemaphoreType.DMA((size - 1,)),
            pltpu.SemaphoreType.DMA((size - 1,)),
            pltpu.SemaphoreType.DMA((1,)),
        ]
    return pl.pallas_call(
        functools.partial(exchange_kernel, kinds, sizes),
        out_shape=tuple(shapes),
        in_specs=[pl.BlockSpec(memory_space=pl.ANY)] * len(items),
        out_specs=tuple(pl.BlockSpec(memory_space=pl.ANY) for _ in items),
        scratch_shapes=scratch,
        compiler_params=pltpu.CompilerParams(collective_id=number, has_side_effects=True),
        name=f"exchange_{number}",
    )(*(array for array, _, _ in items))


def greet(sizes):
    d, f, e = lax.axis_index("dp"), lax.axis_index("fsdp"), lax.axis_index("expert")
    levels = sizes["expert"] // 2
    y, c = e // 2, lax.rem(e, 2)
    barrier = pltpu.get_barrier_semaphore()
    others = []
    for k in range(1, sizes["dp"]):
        others.append({"dp": lax.rem(d + k, sizes["dp"])})
    for k in range(1, sizes["fsdp"]):
        others.append({"fsdp": lax.rem(f + k, sizes["fsdp"])})
    for k in range(1, levels):
        others.append({"expert": lax.rem(y + k, levels) * 2 + c})
    others.append({"expert": y * 2 + 1 - c})
    for other in others:
        pl.semaphore_signal(barrier, inc=1, device_id=other, device_id_type=MESH)
    pl.semaphore_wait(barrier, len(others))
    return d, f, e, y, c


class Sender:
    def __init__(self, send, recv):
        self.send, self.recv, self.next = send, recv, 0

    def __call__(self, source, target, device):
        copy = pltpu.make_async_remote_copy(
            src_ref=source,
            dst_ref=target,
            send_sem=self.send.at[self.next],
            recv_sem=self.recv.at[self.next],
            device_id=device,
            device_id_type=MESH,
        )
        self.next += 1
        copy.start()
        return copy


def project_kernel(
    sizes, att_ref, w_ref, out, tokens, weight, part, one, two, r1, r2, r3, send, recv, local
):
    fs, levels = sizes["fsdp"], sizes["expert"] // 2
    loads = [
        pltpu.make_async_copy(w_ref, weight, local.at[0]),
        pltpu.make_async_copy(att_ref, tokens.at[0], local.at[1]),
    ]
    for copy in loads:
        copy.start()
    d, f, e, y, c = greet(sizes)
    go = Sender(send, recv)
    width = w_ref.shape[1]
    sub = out.shape[0]
    gathers = [None]
    for k in range(1, fs):
        gathers.append(go(att_ref, tokens.at[k], {"fsdp": lax.rem(f + k, fs)}))
    for copy in loads:
        copy.wait()
    flying = {}

    def owner(k):
        return lax.rem(f - k + fs, fs)

    def finish(phase, k):
        for copy in flying.pop((phase, k)):
            copy.wait()

    def make(k):
        if k > 0:
            gathers[k].wait()
        product = jnp.dot(tokens[k], weight[...], preferred_element_type=jnp.float32)
        part[k] = product.reshape(levels, 2, sub, width)
        flying[0, k] = [go(part.at[k, :, 1 - c], r1.at[k], {"expert": y * 2 + 1 - c})]

    def after_chip(k):
        finish(0, k)
        one[k] = part[k, :, c] + r1[k]
        copies = []
        for m in range(1, levels):
            to = lax.rem(y + m, levels)
            copies.append(go(one.at[k, to], r2.at[k, m - 1], {"expert": to * 2 + c}))
        flying[1, k] = copies

    def after_level(k):
        finish(1, k)
        total = one[k, y]
        for m in range(levels - 1):
            total += r2[k, m]
        two[k] = total
        flying[2, k] = []
        if k > 0:
            flying[2, k].append(go(two.at[k], r3.at[k - 1], {"fsdp": owner(k)}))

    stages = (make, after_chip, after_level)
    for step in range(fs + len(stages) - 1):
        for age, stage in enumerate(stages):
            if 0 <= step - age < fs:
                stage(step - age)
    for k in range(fs):
        finish(2, k)
        source = lax.rem(f + k, fs)
        columns = pl.ds(pl.multiple_of(source * width, 128), width)
        out[:, columns] = two[0] if k == 0 else r3[k - 1]


def project(sizes, number, attended, out_weight, sub):
    fs, levels = sizes["fsdp"], sizes["expert"] // 2
    rows, inner = attended.shape
    width = out_weight.shape[1]
    wide = jnp.float32
    sems = (fs - 1) + fs + fs * (levels - 1) + (fs - 1)
    return pl.pallas_call(
        functools.partial(project_kernel, sizes),
        out_shape=jax.ShapeDtypeStruct((sub, fs * width), wide),
        in_specs=[pl.BlockSpec(memory_space=pl.ANY)] * 2,
        out_specs=pl.BlockSpec(memory_space=pltpu.VMEM),
        scratch_shapes=[
            pltpu.VMEM((fs, rows, inner), attended.dtype),
            pltpu.VMEM((inner, width), out_weight.dtype),
            pltpu.VMEM((fs, levels, 2, sub, width), wide),
            pltpu.VMEM((fs, levels, sub, width), wide),
            pltpu.VMEM((fs, sub, width), wide),
            pltpu.VMEM((fs, levels, sub, width), wide),
            pltpu.VMEM((fs, levels - 1, sub, width), wide),
            pltpu.VMEM((fs - 1, sub, width), wide),
            pltpu.SemaphoreType.DMA((sems,)),
            pltpu.SemaphoreType.DMA((sems,)),
            pltpu.SemaphoreType.DMA((2,)),
        ],
        compiler_params=pltpu.CompilerParams(
            collective_id=number, has_side_effects=True, vmem_limit_bytes=32 << 20
        ),
        name="project",
    )(attended, out_weight)


def flat_rows(block, rows):
    if block.shape[-2] % 16 == 0:
        return block.reshape(rows, block.shape[-1])
    return block.astype(jnp.float32).reshape(rows, block.shape[-1]).astype(block.dtype)


def open_rows(block, lead):
    if lead[-1] % 16 == 0:
        return block.astype(jnp.bfloat16).reshape(lead + block.shape[-1:])
    return block.reshape(lead + block.shape[-1:]).astype(jnp.bfloat16)


def spread_kernel(
    sizes, pieces, x_ref, g_ref, gate_ref, up_ref, hidden, gates,
    rows, gate_w, up_w, gate_sum, up_sum, send, recv, local, weight_sems,
):
    dps, fs, levels = sizes["dp"], sizes["fsdp"], sizes["expert"] // 2
    place = (
        lax.axis_index("dp"),
        lax.axis_index("fsdp"),
        lax.axis_index("expert") // 2,
        lax.rem(lax.axis_index("expert"), 2),
    )
    own = [
        pltpu.make_async_copy(x_ref, rows.at[place], local.at[0]),
        pltpu.make_async_copy(g_ref, gates.at[place], local.at[1]),
    ]
    for copy in own:
        copy.start()
    wide = x_ref.shape[-1] // pieces
    half = wide // 2
    loads = []
    for j in range(pieces):
        cols = pl.ds(j * wide, wide)
        pair = [
            pltpu.make_async_copy(gate_ref.at[0, :, cols], gate_w.at[:, cols], weight_sems.at[2 * j]),
            pltpu.make_async_copy(up_ref.at[0, :, cols], up_w.at[:, cols], weight_sems.at[2 * j + 1]),
        ]
        loads.append(pair)
    d, f, e, y, c = greet(sizes)
    go = Sender(send, recv)
    flying = {}

    def start(phase, j):
        low, high = pl.ds(j * wide, half), pl.ds(j * wide + half, half)
        full = pl.ds(j * wide, wide)
        copies = []
        if phase == 0:
            for k in range(1, fs):
                to = {"fsdp": lax.rem(f + k, fs)}
                copies.append(go(x_ref.at[:, full], rows.at[d, f, y, c, :, full], to))
                if j == 0:
                    copies.append(go(g_ref, gates.at[d, f, y, c], to))
        elif phase == 1:
            for k in range(1, dps):
                to = {"dp": lax.rem(d + k, dps)}
                block = rows.at[d, :, y, c, :, low]
                copies.append(go(block, block, to))
                if j == 0:
                    block = gates.at[d, :, y, c]
                    copies.append(go(block, block, to))
            for k in range(1, levels):
                to = {"expert": lax.rem(y + k, levels) * 2 + c}
                block = rows.at[d, :, y, c, :, high]
                copies.append(go(block, block, to))
        elif phase == 2:
            for k in range(1, levels):
                to = {"expert": lax.rem(y + k, levels) * 2 + c}
                block = rows.at[:, :, y, c, :, low]
                copies.append(go(block, block, to))
                if j == 0:
                    block = gates.at[:, :, y, c]
                    copies.append(go(block, block, to))
            for k in range(1, dps):
                to = {"dp": lax.rem(d + k, dps)}
                block = rows.at[d, :, :, c, :, high]
                copies.append(go(block, block, to))
        else:
            to = {"expert": y * 2 + 1 - c}
            block = rows.at[:, :, :, c, :, full]
            copies.append(go(block, block, to))
            if j == 0:
                block = gates.at[:, :, :, c]
                copies.append(go(block, block, to))
        flying[phase, j] = copies

    def finish(phase, j):
        for copy in flying.pop((phase, j)):
            copy.wait()

    for j in range(pieces):
        start(0, j)
    for pair in loads:
        for copy in pair:
            copy.start()
    for copy in own:
        copy.wait()
    every, units = hidden.shape
    tile = 256 if units % 256 == 0 else 128
    for step in range(pieces + 3):
        for phase in (3, 2, 1):
            j = step - phase + 1
            if 0 <= j < pieces:
                finish(phase - 1, j)
                start(phase, j)
        j = step - 3
        if j < 0:
            continue
        finish(3, j)
        for copy in loads[j]:
            copy.wait()

        @pl.loop(0, units // tile)
        def _(i, j=j):
            full = pl.ds(j * wide, wide)
            picked = pl.ds(pl.multiple_of(i * tile, tile), tile)
            block = flat_rows(rows[:, :, :, :, :, full], every)
            last = (((1,), (1,)), ((), ()))
            g = lax.dot_general(
                block, gate_w[picked, full], last, preferred_element_type=jnp.float32
            )
            u = lax.dot_general(block, up_w[picked, full], last, preferred_element_type=jnp.float32)
            if j > 0:
                g += gate_sum[:, picked]
                u += up_sum[:, picked]
            if j < pieces - 1:
                gate_sum[:, picked] = g
                up_sum[:, picked] = u
            else:
                hidden[:, picked] = (g / (1.0 + jnp.exp(-g)) * u).astype(hidden.dtype)


def spread(sizes, number, rows, shares, gate_weight, up_weight, pieces=4):
    dps, fs, levels = sizes["dp"], sizes["fsdp"], sizes["expert"] // 2
    lead = (dps, fs, levels, 2)
    sub, width = rows.shape
    every = dps * fs * levels * 2 * sub
    units = gate_weight.shape[1]
    gate_copies = (fs - 1) + (dps - 1) + (levels - 1) + 1
    sems = pieces * ((fs - 1) + 2 * (dps - 1) + 2 * (levels - 1) + 1) + gate_copies
    return pl.pallas_call(
        functools.partial(spread_kernel, sizes, pieces),
        out_shape=(
            jax.ShapeDtypeStruct((every, units), jnp.bfloat16),
            jax.ShapeDtypeStruct(lead + shares.shape, shares.dtype),
        ),
        in_specs=[pl.BlockSpec(memory_space=pl.ANY)] * 4,
        out_specs=(pl.BlockSpec(memory_space=pltpu.VMEM), pl.BlockSpec(memory_space=pl.ANY)),
        scratch_shapes=[
            pltpu.VMEM(lead + rows.shape, rows.dtype),
            pltpu.VMEM((units, width), rows.dtype),
            pltpu.VMEM((units, width), rows.dtype),
            pltpu.VMEM((every, units), jnp.float32),
            pltpu.VMEM((every, units), jnp.float32),
            pltpu.SemaphoreType.DMA((sems,)),
            pltpu.SemaphoreType.DMA((sems,)),
            pltpu.SemaphoreType.DMA((2,)),
            pltpu.SemaphoreType.DMA((2 * pieces,)),
        ],
        compiler_params=pltpu.CompilerParams(
            collective_id=number, has_side_effects=True, vmem_limit_bytes=56 << 20
        ),
        name="spread",
    )(rows, shares, gate_weight, up_weight)


def collect_kernel(
    sizes, pieces, hidden, share, down_ref, out,
    terms, down_w, one, two_a, two_b, three, r1, r2a, r2b, r3a, r3b, r4, send, recv, weight_sems,
):
    dps, fs, levels = sizes["dp"], sizes["fsdp"], sizes["expert"] // 2
    sub, width = out.shape
    wide = width // pieces
    half = wide // 2
    loads = []
    for j in range(pieces):
        cols = pl.ds(j * wide, wide)
        copy = pltpu.make_async_copy(down_ref.at[0, :, cols], down_w.at[:, cols], weight_sems.at[j])
        copy.start()
        loads.append(copy)
    d, f, e, y, c = greet(sizes)
    go = Sender(send, recv)
    flying = {}
    wider = jnp.float32
    tile = 256

    def finish(phase, j):
        for copy in flying.pop((phase, j)):
            copy.wait()

    def make(j):
        loads[j].wait()

        @pl.loop(0, wide // tile)
        def _(i):
            picked = pl.ds(pl.multiple_of(j * wide + i * tile, tile), tile)
            product = jnp.dot(hidden[...], down_w[:, picked], preferred_element_type=wider)
            terms[:, :, :, :, :, picked] = open_rows(
                product * share[...], (dps, fs, levels, 2, sub)
            )

        full = pl.ds(j * wide, wide)
        flying[0, j] = [
            go(terms.at[:, :, :, 1 - c, :, full], r1.at[:, :, :, :, full], {"expert": y * 2 + 1 - c})
        ]

    def after_chip(j):
        finish(0, j)
        low, high = pl.ds(j * wide, half), pl.ds(j * wide + half, half)
        full = pl.ds(j * wide, wide)
        narrow = pl.ds(j * half, half)

        @pl.loop(0, dps * fs * levels)
        def _(i):
            p, q, r = i // (fs * levels), lax.rem(i // levels, fs), lax.rem(i, levels)
            one[p, q, r, :, full] = (
                terms[p, q, r, c, :, full].astype(wider) + r1[p, q, r, :, full].astype(wider)
            ).astype(one.dtype)

        copies = []
        for k in range(1, dps):
            to = lax.rem(d + k, dps)
            copies.append(
                go(one.at[to, :, :, :, low], r2a.at[k - 1, :, :, :, narrow], {"dp": to})
            )
        for k in range(1, levels):
            to = lax.rem(y + k, levels)
            copies.append(
                go(one.at[:, :, to, :, high], r2b.at[k - 1, :, :, :, narrow], {"expert": to * 2 + c})
            )
        flying[1, j] = copies

    def after_first(j):
        finish(1, j)
        low, high = pl.ds(j * wide, half), pl.ds(j * wide + half, half)
        narrow = pl.ds(j * half, half)

        @pl.loop(0, fs * levels)
        def _(i):
            q, r = i // levels, lax.rem(i, levels)
            total = one[d, q, r, :, low].astype(wider)
            for k in range(dps - 1):
                total += r2a[k, q, r, :, narrow].astype(wider)
            two_a[q, r, :, narrow] = total.astype(two_a.dtype)

        @pl.loop(0, dps * fs)
        def _(i):
            p, q = i // fs, lax.rem(i, fs)
            total = one[p, q, y, :, high].astype(wider)
            for k in range(levels - 1):
                total += r2b[k, p, q, :, narrow].astype(wider)
            two_b[p, q, :, narrow] = total.astype(two_b.dtype)

        copies = []
        for k in range(1, levels):
            to = lax.rem(y + k, levels)
            copies.append(
                go(two_a.at[:, to, :, narrow], r3a.at[k - 1, :, :, narrow], {"expert": to * 2 + c})
            )
        for k in range(1, dps):
            to = lax.rem(d + k, dps)
            copies.append(go(two_b.at[to, :, :, narrow], r3b.at[k - 1, :, :, narrow], {"dp": to}))
        flying[2, j] = copies

    def after_second(j):
        finish(2, j)
        low, high = pl.ds(j * wide, half), pl.ds(j * wide + half, half)
        full = pl.ds(j * wide, wide)
        narrow = pl.ds(j * half, half)

        @pl.loop(0, fs)
        def _(q):
            total = two_a[q, y, :, narrow].astype(wider)
            for k in range(levels - 1):
                total += r3a[k, q, :, narrow].astype(wider)
            three[q, :, low] = total.astype(three.dtype)
            total = two_b[d, q, :, narrow].astype(wider)
            for k in range(dps - 1):
                total += r3b[k, q, :, narrow].astype(wider)
            three[q, :, high] = total.astype(three.dtype)

        copies = []
        for k in range(1, fs):
            to = lax.rem(f + k, fs)
            copies.append(go(three.at[to, :, full], r4.at[k - 1, :, full], {"fsdp": to}))
        flying[3, j] = copies

    def after_third(j):
        finish(3, j)
        full = pl.ds(j * wide, wide)
        total = three[f, :, full].astype(wider)
        for k in range(fs - 1):
            total += r4[k, :, full].astype(wider)
        out[:, full] = total

    stages = (make, after_chip, after_first, after_second, after_third)
    for step in range(pieces + len(stages) - 1):
        for age, stage in enumerate(stages):
            if 0 <= step - age < pieces:
                stage(step - age)


def collect(sizes, number, hidden, share, down_weight, sub, pieces=4):
    dps, fs, levels = sizes["dp"], sizes["fsdp"], sizes["expert"] // 2
    units, width = down_weight.shape[1:]
    half = width // 2
    kind = jnp.bfloat16
    sems = pieces * (1 + 2 * (dps - 1) + 2 * (levels - 1) + (fs - 1))
    return pl.pallas_call(
        functools.partial(collect_kernel, sizes, pieces),
        out_shape=jax.ShapeDtypeStruct((sub, width), jnp.float32),
        in_specs=[
            pl.BlockSpec(memory_space=pltpu.VMEM),
            pl.BlockSpec(memory_space=pltpu.VMEM),
            pl.BlockSpec(memory_space=pl.ANY),
        ],
        out_specs=pl.BlockSpec(memory_space=pltpu.VMEM),
        scratch_shapes=[
            pltpu.VMEM((dps, fs, levels, 2, sub, width), kind),
            pltpu.VMEM((units, width), kind),
            pltpu.VMEM((dps, fs, levels, sub, width), kind),
            pltpu.VMEM((fs, levels, sub, half), kind),
            pltpu.VMEM((dps, fs, sub, half), kind),
            pltpu.VMEM((fs, sub, width), kind),
            pltpu.VMEM((dps, fs, levels, sub, width), kind),
            pltpu.VMEM((dps - 1, fs, levels, sub, half), kind),
            pltpu.VMEM((levels - 1, dps, fs, sub, half), kind),
            pltpu.VMEM((levels - 1, fs, sub, half), kind),
            pltpu.VMEM((dps - 1, fs, sub, half), kind),
            pltpu.VMEM((fs - 1, sub, width), kind),
            pltpu.SemaphoreType.DMA((sems,)),
            pltpu.SemaphoreType.DMA((sems,)),
            pltpu.SemaphoreType.DMA((pieces,)),
        ],
        compiler_params=pltpu.CompilerParams(
            collective_id=number, has_side_effects=True, vmem_limit_bytes=56 << 20
        ),
        name="collect",
    )(hidden, share, down_weight)


def local(
    sizes,
    window,
    attention_gain,
    query_weight,
    key_weight,
    value_weight,
    out_weight,
    cache_keys,
    cache_values,
    occluded,
    feedforward_gain,
    router_weight,
    chosen_experts,
    gate_weight,
    up_weight,
    down_weight,
):
    dps, fs, es = sizes["dp"], sizes["fsdp"], sizes["expert"]
    token_rows, width = window.shape
    d, f, e = lax.axis_index("dp"), lax.axis_index("fsdp"), lax.axis_index("expert")
    query_width = query_weight.shape[1]
    key_width = key_weight.shape[1]
    query_heads = query_width // HD
    key_heads = key_width // HD
    grouping = query_heads // key_heads
    window_rows = token_rows * fs
    prefix_rows = cache_keys.shape[0] * dps
    score_scale = HD ** (-0.5)
    part = token_rows // dps
    sub = token_rows // es

    own_rows = lax.dynamic_slice_in_dim(window, d * part, part, 0)
    normed = rms_norm(own_rows, attention_gain)
    flags = occluded.astype(jnp.float32).T
    (columns,) = exchange(sizes, 0, (normed, "columns", ("fsdp",)))
    columns = columns.reshape(fs * part, width // fs)
    sums = jnp.concatenate(
        [
            jnp.dot(columns, weight, preferred_element_type=jnp.float32)
            for weight in (query_weight, key_weight, value_weight)
        ],
        axis=1,
    )
    sums, keys_block, values_block, flags_block = exchange(
        sizes,
        1,
        (sums.reshape(fs, part, -1), "rows", ("fsdp",)),
        (cache_keys, "gather", ("dp",)),
        (cache_values, "gather", ("dp",)),
        (flags, "gather", ("dp",)),
    )
    sums = jnp.sum(sums, axis=0)
    positions = prefix_rows + f * token_rows + d * part + jnp.arange(part, dtype=jnp.int32)
    rotated = rotate(
        sums[:, : query_width + key_width].reshape(part, query_heads + key_heads, HD), positions
    ).astype(jnp.bfloat16)
    queries = rotated[:, :query_heads].reshape(part, query_width)
    fresh = jnp.concatenate(
        [
            rotated[:, query_heads:].reshape(part, key_width),
            sums[:, query_width + key_width :].astype(jnp.bfloat16),
        ],
        axis=1,
    )
    queries, fresh = exchange(
        sizes, 2, (queries, "gather", ("dp",)), (fresh, "gather", ("fsdp", "dp"))
    )
    fresh = fresh.reshape(window_rows, 2 * key_width)
    query_grid = queries.reshape(token_rows, key_heads, grouping, HD)
    all_keys = jnp.concatenate(
        [keys_block.reshape(prefix_rows, key_width), fresh[:, :key_width]], axis=0
    ).reshape(prefix_rows + window_rows, key_heads, HD)
    all_values = jnp.concatenate(
        [values_block.reshape(prefix_rows, key_width), fresh[:, key_width:]], axis=0
    ).reshape(prefix_rows + window_rows, key_heads, HD)
    scores = (
        jnp.einsum("tkgd,nkd->kgtn", query_grid, all_keys, preferred_element_type=jnp.float32)
        * score_scale
    )
    seen = lax.dynamic_slice_in_dim(flags_block, d, 1, 1).reshape(prefix_rows) == 0
    causal = (
        jnp.arange(window_rows)[None, :]
        <= (f * token_rows + jnp.arange(token_rows))[:, None]
    )
    visible = jnp.concatenate(
        [jnp.broadcast_to(seen[None, :], (token_rows, prefix_rows)), causal], axis=1
    )
    masked = jnp.where(visible, scores, floor_score)
    top = jnp.max(masked, axis=-1, keepdims=True)
    weights = jnp.exp(masked - top)
    totals = jnp.sum(weights, axis=-1)
    heads = jnp.einsum(
        "kgtn,nkd->tkgd",
        weights.astype(jnp.bfloat16),
        all_values,
        preferred_element_type=jnp.float32,
    ) / totals.transpose(2, 0, 1)[..., None]
    attended = heads.reshape(token_rows, query_width).astype(jnp.bfloat16)

    projected = project(sizes, 3, attended, out_weight, sub)
    residual = lax.dynamic_slice_in_dim(window, e * sub, sub, 0).astype(jnp.float32) + projected
    normed_mix = rms_norm(residual, feedforward_gain)
    logits = jnp.dot(normed_mix, router_weight, preferred_element_type=jnp.float32)
    picks = lax.dynamic_slice_in_dim(chosen_experts.reshape(token_rows, TOP), e * sub, sub, 0)
    experts = router_weight.shape[1]
    matches = picks[:, :, None] == jnp.arange(experts, dtype=jnp.int32)[None, None, :]
    picked = jnp.sum(jnp.where(matches, logits[:, None, :], 0.0), axis=-1)
    gate_shares = jax.nn.sigmoid(picked - picked[:, ::-1])
    lanes = picks[:, :, None] == jnp.arange(128, dtype=jnp.int32)[None, None, :]
    shares = jnp.sum(jnp.where(lanes, gate_shares[:, :, None], 0.0), axis=1)

    hidden, shares = spread(sizes, 6, normed_mix, shares, gate_weight, up_weight)
    share = lax.dynamic_slice_in_dim(shares.reshape(dps * window_rows, 128), e, 1, 1)
    mixture = collect(sizes, 7, hidden, share, down_weight, sub)
    (whole,) = exchange(
        sizes, 8, ((residual + mixture).astype(jnp.bfloat16), "gather", ("expert",))
    )
    return whole.reshape(1, token_rows, width)


def solution(mesh):
    sizes = dict(mesh.shape)
    placed = (
        P("fsdp", None),
        P(),
        P("fsdp", "expert"),
        P("fsdp", "expert"),
        P("fsdp", "expert"),
        P("expert", "fsdp"),
        P("dp", "expert"),
        P("dp", "expert"),
        P("dp", None),
        P(),
        P(),
        P("dp", "fsdp", None),
        P("expert", ("dp", "fsdp"), None),
        P("expert", ("dp", "fsdp"), None),
        P("expert", ("dp", "fsdp"), None),
    )
    return jax.shard_map(
        functools.partial(local, sizes),
        mesh=mesh,
        in_specs=placed,
        out_specs=P("dp", "fsdp", None),
        check_vma=False,
    )
```

```python
import functools

import jax
import jax.numpy as jnp
from jax import lax
from jax.experimental import pallas as pl
from jax.experimental.pallas import tpu as pltpu
from jax.sharding import PartitionSpec as P

HD = 128
TOP = 2

epsilon = 1e-05
rope_base = 1000000.0
floor_score = -1e30
MESH = pl.DeviceIdType.MESH


def rms_norm(values, scales):
    widened = values.astype(jnp.float32)
    inverse = lax.rsqrt(jnp.mean(widened * widened, axis=-1, keepdims=True) + epsilon)
    return (widened * inverse * scales).astype(jnp.bfloat16)


def rotate(vectors, positions):
    halfway = vectors.shape[-1] // 2
    powers = jnp.arange(halfway, dtype=jnp.float32) * (2.0 / vectors.shape[-1])
    frequency = rope_base ** (-powers)
    angles = positions.astype(jnp.float32)[:, None] * frequency[None, :]
    cosine = jnp.cos(angles)[:, None, :]
    sine_part = jnp.sin(angles)[:, None, :]
    former = vectors[..., :halfway]
    latter = vectors[..., halfway:]
    return jnp.concatenate(
        [former * cosine - latter * sine_part, latter * cosine + former * sine_part], axis=-1
    )


def linear_place(axes, sizes):
    place = 0
    for axis in axes:
        place = place * sizes[axis] + lax.axis_index(axis)
    return place


def coordinates(axes, sizes, place):
    found = {}
    for axis in reversed(axes):
        found[axis] = lax.rem(place, sizes[axis])
        place = place // sizes[axis]
    return found


def count(axes, sizes):
    total = 1
    for axis in axes:
        total *= sizes[axis]
    return total


def source_part(kind, ref, to):
    if kind == "gather":
        return ref
    if kind == "rows":
        return ref.at[to]
    if kind == "second":
        return ref.at[:, to]
    if kind == "rows_to_columns":
        return ref.at[to]
    raise ValueError(kind)


def exchange_kernel(kinds, sizes, *refs):
    n = len(kinds)
    inputs, outputs, sems = refs[:n], refs[n : 2 * n], refs[2 * n :]
    barrier = pltpu.get_barrier_semaphore()
    total = 0
    for _, axes in kinds:
        size = count(axes, sizes)
        here = linear_place(axes, sizes)
        for k in range(1, size):
            to = coordinates(axes, sizes, lax.rem(here + k, size))
            pl.semaphore_signal(barrier, inc=1, device_id=to, device_id_type=MESH)
        total += size - 1
    local_copies = []

    def landing(kind, out, here, width):
        if kind == "rows_to_columns":
            return out.at[:, pl.ds(pl.multiple_of(here * width, 128), width)]
        return out.at[here]

    def part(kind, ref, to, size):
        if kind == "columns":
            width = ref.shape[1] // size
            return ref.at[:, pl.ds(pl.multiple_of(to * width, 128), width)]
        return source_part(kind, ref, to)

    for i, (kind, axes) in enumerate(kinds):
        size = count(axes, sizes)
        here = linear_place(axes, sizes)
        width = inputs[i].shape[-1]
        own = pltpu.make_async_copy(
            part(kind, inputs[i], here, size),
            landing(kind, outputs[i], here, width),
            sems[3 * i + 2].at[0],
        )
        own.start()
        local_copies.append(own)
    pl.semaphore_wait(barrier, total)
    copies = []
    for i, (kind, axes) in enumerate(kinds):
        size = count(axes, sizes)
        here = linear_place(axes, sizes)
        width = inputs[i].shape[-1]
        for k in range(1, size):
            place = lax.rem(here + k, size)
            copy = pltpu.make_async_remote_copy(
                src_ref=part(kind, inputs[i], place, size),
                dst_ref=landing(kind, outputs[i], here, width),
                send_sem=sems[3 * i].at[k - 1],
                recv_sem=sems[3 * i + 1].at[k - 1],
                device_id=coordinates(axes, sizes, place),
                device_id_type=MESH,
            )
            copy.start()
            copies.append(copy)
    for own in local_copies:
        own.wait()
    for copy in copies:
        copy.wait()


def exchange(sizes, number, *items):
    kinds = tuple((kind, axes) for _, kind, axes in items)
    shapes, scratch = [], []
    for array, kind, axes in items:
        size = count(axes, sizes)
        if kind == "gather":
            shape = (size,) + array.shape
        elif kind == "rows":
            shape = array.shape
        elif kind == "second":
            shape = (size, array.shape[0]) + array.shape[2:]
        elif kind == "columns":
            shape = (size, array.shape[0], array.shape[1] // size)
        else:
            shape = (array.shape[1], size * array.shape[2])
        shapes.append(jax.ShapeDtypeStruct(shape, array.dtype))
        scratch += [
            pltpu.SemaphoreType.DMA((size - 1,)),
            pltpu.SemaphoreType.DMA((size - 1,)),
            pltpu.SemaphoreType.DMA((1,)),
        ]
    return pl.pallas_call(
        functools.partial(exchange_kernel, kinds, sizes),
        out_shape=tuple(shapes),
        in_specs=[pl.BlockSpec(memory_space=pl.ANY)] * len(items),
        out_specs=tuple(pl.BlockSpec(memory_space=pl.ANY) for _ in items),
        scratch_shapes=scratch,
        compiler_params=pltpu.CompilerParams(collective_id=number, has_side_effects=True),
        name=f"exchange_{number}",
    )(*(array for array, _, _ in items))


def greet(sizes):
    d, f, e = lax.axis_index("dp"), lax.axis_index("fsdp"), lax.axis_index("expert")
    levels = sizes["expert"] // 2
    y, c = e // 2, lax.rem(e, 2)
    barrier = pltpu.get_barrier_semaphore()
    others = []
    for k in range(1, sizes["dp"]):
        others.append({"dp": lax.rem(d + k, sizes["dp"])})
    for k in range(1, sizes["fsdp"]):
        others.append({"fsdp": lax.rem(f + k, sizes["fsdp"])})
    for k in range(1, levels):
        others.append({"expert": lax.rem(y + k, levels) * 2 + c})
    others.append({"expert": y * 2 + 1 - c})
    for other in others:
        pl.semaphore_signal(barrier, inc=1, device_id=other, device_id_type=MESH)
    pl.semaphore_wait(barrier, len(others))
    return d, f, e, y, c


class Sender:
    def __init__(self, send, recv):
        self.send, self.recv, self.next = send, recv, 0

    def __call__(self, source, target, device):
        copy = pltpu.make_async_remote_copy(
            src_ref=source,
            dst_ref=target,
            send_sem=self.send.at[self.next],
            recv_sem=self.recv.at[self.next],
            device_id=device,
            device_id_type=MESH,
        )
        self.next += 1
        copy.start()
        return copy


def project_kernel(
    sizes, att_ref, w_ref, out, tokens, weight, part, one, two, r1, r2, r3, send, recv, local
):
    fs, levels = sizes["fsdp"], sizes["expert"] // 2
    loads = [
        pltpu.make_async_copy(w_ref, weight, local.at[0]),
        pltpu.make_async_copy(att_ref, tokens.at[0], local.at[1]),
    ]
    for copy in loads:
        copy.start()
    d, f, e, y, c = greet(sizes)
    go = Sender(send, recv)
    width = w_ref.shape[1]
    sub = out.shape[0]
    gathers = [None]
    for k in range(1, fs):
        gathers.append(go(att_ref, tokens.at[k], {"fsdp": lax.rem(f + k, fs)}))
    for copy in loads:
        copy.wait()
    flying = {}

    def owner(k):
        return lax.rem(f - k + fs, fs)

    def finish(phase, k):
        for copy in flying.pop((phase, k)):
            copy.wait()

    def make(k):
        if k > 0:
            gathers[k].wait()
        product = jnp.dot(tokens[k], weight[...], preferred_element_type=jnp.float32)
        part[k] = product.reshape(levels, 2, sub, width)
        flying[0, k] = [go(part.at[k, :, 1 - c], r1.at[k], {"expert": y * 2 + 1 - c})]

    def after_chip(k):
        finish(0, k)
        one[k] = part[k, :, c] + r1[k]
        copies = []
        for m in range(1, levels):
            to = lax.rem(y + m, levels)
            copies.append(go(one.at[k, to], r2.at[k, m - 1], {"expert": to * 2 + c}))
        flying[1, k] = copies

    def after_level(k):
        finish(1, k)
        total = one[k, y]
        for m in range(levels - 1):
            total += r2[k, m]
        two[k] = total
        flying[2, k] = []
        if k > 0:
            flying[2, k].append(go(two.at[k], r3.at[k - 1], {"fsdp": owner(k)}))

    stages = (make, after_chip, after_level)
    for step in range(fs + len(stages) - 1):
        for age, stage in enumerate(stages):
            if 0 <= step - age < fs:
                stage(step - age)
    for k in range(fs):
        finish(2, k)
        source = lax.rem(f + k, fs)
        columns = pl.ds(pl.multiple_of(source * width, 128), width)
        out[:, columns] = two[0] if k == 0 else r3[k - 1]


def project(sizes, number, attended, out_weight, sub):
    fs, levels = sizes["fsdp"], sizes["expert"] // 2
    rows, inner = attended.shape
    width = out_weight.shape[1]
    wide = jnp.float32
    sems = (fs - 1) + fs + fs * (levels - 1) + (fs - 1)
    return pl.pallas_call(
        functools.partial(project_kernel, sizes),
        out_shape=jax.ShapeDtypeStruct((sub, fs * width), wide),
        in_specs=[pl.BlockSpec(memory_space=pl.ANY)] * 2,
        out_specs=pl.BlockSpec(memory_space=pltpu.VMEM),
        scratch_shapes=[
            pltpu.VMEM((fs, rows, inner), attended.dtype),
            pltpu.VMEM((inner, width), out_weight.dtype),
            pltpu.VMEM((fs, levels, 2, sub, width), wide),
            pltpu.VMEM((fs, levels, sub, width), wide),
            pltpu.VMEM((fs, sub, width), wide),
            pltpu.VMEM((fs, levels, sub, width), wide),
            pltpu.VMEM((fs, levels - 1, sub, width), wide),
            pltpu.VMEM((fs - 1, sub, width), wide),
            pltpu.SemaphoreType.DMA((sems,)),
            pltpu.SemaphoreType.DMA((sems,)),
            pltpu.SemaphoreType.DMA((2,)),
        ],
        compiler_params=pltpu.CompilerParams(
            collective_id=number, has_side_effects=True, vmem_limit_bytes=32 << 20
        ),
        name="project",
    )(attended, out_weight)


def flat_rows(block, rows):
    if block.shape[-2] % 16 == 0:
        return block.reshape(rows, block.shape[-1])
    return block.astype(jnp.float32).reshape(rows, block.shape[-1]).astype(block.dtype)


def open_rows(block, lead):
    if lead[-1] % 16 == 0:
        return block.astype(jnp.bfloat16).reshape(lead + block.shape[-1:])
    return block.reshape(lead + block.shape[-1:]).astype(jnp.bfloat16)


def spread_kernel(
    sizes, pieces, x_ref, g_ref, gate_ref, up_ref, hidden, gates,
    rows, gate_w, up_w, gate_sum, up_sum, send, recv, local, weight_sems,
):
    dps, fs, levels = sizes["dp"], sizes["fsdp"], sizes["expert"] // 2
    place = (
        lax.axis_index("dp"),
        lax.axis_index("fsdp"),
        lax.axis_index("expert") // 2,
        lax.rem(lax.axis_index("expert"), 2),
    )
    own = [
        pltpu.make_async_copy(x_ref, rows.at[place], local.at[0]),
        pltpu.make_async_copy(g_ref, gates.at[place], local.at[1]),
    ]
    for copy in own:
        copy.start()
    wide = x_ref.shape[-1] // pieces
    half = wide // 2
    loads = []
    for j in range(pieces):
        cols = pl.ds(j * wide, wide)
        pair = [
            pltpu.make_async_copy(gate_ref.at[0, :, cols], gate_w.at[:, cols], weight_sems.at[2 * j]),
            pltpu.make_async_copy(up_ref.at[0, :, cols], up_w.at[:, cols], weight_sems.at[2 * j + 1]),
        ]
        loads.append(pair)
    d, f, e, y, c = greet(sizes)
    go = Sender(send, recv)
    flying = {}

    def start(phase, j):
        low, high = pl.ds(j * wide, half), pl.ds(j * wide + half, half)
        full = pl.ds(j * wide, wide)
        copies = []
        if phase == 0:
            for k in range(1, fs):
                to = {"fsdp": lax.rem(f + k, fs)}
                copies.append(go(x_ref.at[:, full], rows.at[d, f, y, c, :, full], to))
                if j == 0:
                    copies.append(go(g_ref, gates.at[d, f, y, c], to))
        elif phase == 1:
            for k in range(1, dps):
                to = {"dp": lax.rem(d + k, dps)}
                block = rows.at[d, :, y, c, :, low]
                copies.append(go(block, block, to))
                if j == 0:
                    block = gates.at[d, :, y, c]
                    copies.append(go(block, block, to))
            for k in range(1, levels):
                to = {"expert": lax.rem(y + k, levels) * 2 + c}
                block = rows.at[d, :, y, c, :, high]
                copies.append(go(block, block, to))
        elif phase == 2:
            for k in range(1, levels):
                to = {"expert": lax.rem(y + k, levels) * 2 + c}
                block = rows.at[:, :, y, c, :, low]
                copies.append(go(block, block, to))
                if j == 0:
                    block = gates.at[:, :, y, c]
                    copies.append(go(block, block, to))
            for k in range(1, dps):
                to = {"dp": lax.rem(d + k, dps)}
                block = rows.at[d, :, :, c, :, high]
                copies.append(go(block, block, to))
        else:
            to = {"expert": y * 2 + 1 - c}
            block = rows.at[:, :, :, c, :, full]
            copies.append(go(block, block, to))
            if j == 0:
                block = gates.at[:, :, :, c]
                copies.append(go(block, block, to))
        flying[phase, j] = copies

    def finish(phase, j):
        for copy in flying.pop((phase, j)):
            copy.wait()

    for j in range(pieces):
        start(0, j)
    for pair in loads:
        for copy in pair:
            copy.start()
    for copy in own:
        copy.wait()
    every, units = hidden.shape
    tile = 256 if units % 256 == 0 else 128
    for step in range(pieces + 3):
        for phase in (3, 2, 1):
            j = step - phase + 1
            if 0 <= j < pieces:
                finish(phase - 1, j)
                start(phase, j)
        j = step - 3
        if j < 0:
            continue
        finish(3, j)
        for copy in loads[j]:
            copy.wait()

        @pl.loop(0, units // tile)
        def _(i, j=j):
            full = pl.ds(j * wide, wide)
            picked = pl.ds(pl.multiple_of(i * tile, tile), tile)
            block = flat_rows(rows[:, :, :, :, :, full], every)
            last = (((1,), (1,)), ((), ()))
            g = lax.dot_general(
                block, gate_w[picked, full], last, preferred_element_type=jnp.float32
            )
            u = lax.dot_general(block, up_w[picked, full], last, preferred_element_type=jnp.float32)
            if j > 0:
                g += gate_sum[:, picked]
                u += up_sum[:, picked]
            if j < pieces - 1:
                gate_sum[:, picked] = g
                up_sum[:, picked] = u
            else:
                hidden[:, picked] = (g / (1.0 + jnp.exp(-g)) * u).astype(hidden.dtype)


def spread(sizes, number, rows, shares, gate_weight, up_weight, pieces=4):
    dps, fs, levels = sizes["dp"], sizes["fsdp"], sizes["expert"] // 2
    lead = (dps, fs, levels, 2)
    sub, width = rows.shape
    every = dps * fs * levels * 2 * sub
    units = gate_weight.shape[1]
    gate_copies = (fs - 1) + (dps - 1) + (levels - 1) + 1
    sems = pieces * ((fs - 1) + 2 * (dps - 1) + 2 * (levels - 1) + 1) + gate_copies
    return pl.pallas_call(
        functools.partial(spread_kernel, sizes, pieces),
        out_shape=(
            jax.ShapeDtypeStruct((every, units), jnp.bfloat16),
            jax.ShapeDtypeStruct(lead + shares.shape, shares.dtype),
        ),
        in_specs=[pl.BlockSpec(memory_space=pl.ANY)] * 4,
        out_specs=(pl.BlockSpec(memory_space=pltpu.VMEM), pl.BlockSpec(memory_space=pl.ANY)),
        scratch_shapes=[
            pltpu.VMEM(lead + rows.shape, rows.dtype),
            pltpu.VMEM((units, width), rows.dtype),
            pltpu.VMEM((units, width), rows.dtype),
            pltpu.VMEM((every, units), jnp.float32),
            pltpu.VMEM((every, units), jnp.float32),
            pltpu.SemaphoreType.DMA((sems,)),
            pltpu.SemaphoreType.DMA((sems,)),
            pltpu.SemaphoreType.DMA((2,)),
            pltpu.SemaphoreType.DMA((2 * pieces,)),
        ],
        compiler_params=pltpu.CompilerParams(
            collective_id=number, has_side_effects=True, vmem_limit_bytes=56 << 20
        ),
        name="spread",
    )(rows, shares, gate_weight, up_weight)


def collect_kernel(
    sizes, pieces, hidden, share, residual, down_ref, out,
    final, terms, down_w, one, two_a, two_b, three, r1, r2a, r2b, r3a, r3b, r4, send, recv, weight_sems,
):
    dps, fs, levels = sizes["dp"], sizes["fsdp"], sizes["expert"] // 2
    sub, width = residual.shape
    wide = width // pieces
    half = wide // 2
    loads = []
    for j in range(pieces):
        cols = pl.ds(j * wide, wide)
        copy = pltpu.make_async_copy(down_ref.at[0, :, cols], down_w.at[:, cols], weight_sems.at[j])
        copy.start()
        loads.append(copy)
    d, f, e, y, c = greet(sizes)
    go = Sender(send, recv)
    flying = {}
    wider = jnp.float32
    tile = 256

    def finish(phase, j):
        for copy in flying.pop((phase, j)):
            copy.wait()

    def make(j):
        loads[j].wait()

        @pl.loop(0, wide // tile)
        def _(i):
            picked = pl.ds(pl.multiple_of(j * wide + i * tile, tile), tile)
            product = jnp.dot(hidden[...], down_w[:, picked], preferred_element_type=wider)
            terms[:, :, :, :, :, picked] = open_rows(
                product * share[...], (dps, fs, levels, 2, sub)
            )

        full = pl.ds(j * wide, wide)
        flying[0, j] = [
            go(terms.at[:, :, :, 1 - c, :, full], r1.at[:, :, :, :, full], {"expert": y * 2 + 1 - c})
        ]

    def after_chip(j):
        finish(0, j)
        low, high = pl.ds(j * wide, half), pl.ds(j * wide + half, half)
        full = pl.ds(j * wide, wide)
        narrow = pl.ds(j * half, half)

        @pl.loop(0, dps * fs * levels)
        def _(i):
            p, q, r = i // (fs * levels), lax.rem(i // levels, fs), lax.rem(i, levels)
            one[p, q, r, :, full] = (
                terms[p, q, r, c, :, full].astype(wider) + r1[p, q, r, :, full].astype(wider)
            ).astype(one.dtype)

        copies = []
        for k in range(1, dps):
            to = lax.rem(d + k, dps)
            copies.append(
                go(one.at[to, :, :, :, low], r2a.at[k - 1, :, :, :, narrow], {"dp": to})
            )
        for k in range(1, levels):
            to = lax.rem(y + k, levels)
            copies.append(
                go(one.at[:, :, to, :, high], r2b.at[k - 1, :, :, :, narrow], {"expert": to * 2 + c})
            )
        flying[1, j] = copies

    def after_first(j):
        finish(1, j)
        low, high = pl.ds(j * wide, half), pl.ds(j * wide + half, half)
        narrow = pl.ds(j * half, half)

        @pl.loop(0, fs * levels)
        def _(i):
            q, r = i // levels, lax.rem(i, levels)
            total = one[d, q, r, :, low].astype(wider)
            for k in range(dps - 1):
                total += r2a[k, q, r, :, narrow].astype(wider)
            two_a[q, r, :, narrow] = total.astype(two_a.dtype)

        @pl.loop(0, dps * fs)
        def _(i):
            p, q = i // fs, lax.rem(i, fs)
            total = one[p, q, y, :, high].astype(wider)
            for k in range(levels - 1):
                total += r2b[k, p, q, :, narrow].astype(wider)
            two_b[p, q, :, narrow] = total.astype(two_b.dtype)

        copies = []
        for k in range(1, levels):
            to = lax.rem(y + k, levels)
            copies.append(
                go(two_a.at[:, to, :, narrow], r3a.at[k - 1, :, :, narrow], {"expert": to * 2 + c})
            )
        for k in range(1, dps):
            to = lax.rem(d + k, dps)
            copies.append(go(two_b.at[to, :, :, narrow], r3b.at[k - 1, :, :, narrow], {"dp": to}))
        flying[2, j] = copies

    def after_second(j):
        finish(2, j)
        low, high = pl.ds(j * wide, half), pl.ds(j * wide + half, half)
        full = pl.ds(j * wide, wide)
        narrow = pl.ds(j * half, half)

        @pl.loop(0, fs)
        def _(q):
            total = two_a[q, y, :, narrow].astype(wider)
            for k in range(levels - 1):
                total += r3a[k, q, :, narrow].astype(wider)
            three[q, :, low] = total.astype(three.dtype)
            total = two_b[d, q, :, narrow].astype(wider)
            for k in range(dps - 1):
                total += r3b[k, q, :, narrow].astype(wider)
            three[q, :, high] = total.astype(three.dtype)

        copies = []
        for k in range(1, fs):
            to = lax.rem(f + k, fs)
            copies.append(go(three.at[to, :, full], r4.at[k - 1, :, full], {"fsdp": to}))
        flying[3, j] = copies

    def after_third(j):
        finish(3, j)
        full = pl.ds(j * wide, wide)
        total = three[f, :, full].astype(wider)
        for k in range(fs - 1):
            total += r4[k, :, full].astype(wider)
        final[y, c, :, full] = (residual[:, full] + total).astype(final.dtype)
        block = final.at[y, c, :, full]
        flying[4, j] = [
            go(block, block, {"expert": lax.rem(y + k, levels) * 2 + c}) for k in range(1, levels)
        ]

    def after_sum(j):
        finish(4, j)
        block = final.at[:, c, :, pl.ds(j * wide, wide)]
        flying[5, j] = [go(block, block, {"expert": y * 2 + 1 - c})]

    def after_rows(j):
        finish(5, j)

    stages = (
        make, after_chip, after_first, after_second, after_third, after_sum, after_rows,
    )
    for step in range(pieces + len(stages) - 1):
        for age, stage in enumerate(stages):
            if 0 <= step - age < pieces:
                stage(step - age)
    out[...] = final[...]


def collect(sizes, number, hidden, share, residual, down_weight, pieces=4):
    dps, fs, levels = sizes["dp"], sizes["fsdp"], sizes["expert"] // 2
    units, width = down_weight.shape[1:]
    sub = residual.shape[0]
    half = width // 2
    kind = jnp.bfloat16
    sems = pieces * (2 + 2 * (dps - 1) + 3 * (levels - 1) + (fs - 1))
    return pl.pallas_call(
        functools.partial(collect_kernel, sizes, pieces),
        out_shape=jax.ShapeDtypeStruct((levels, 2, sub, width), kind),
        in_specs=[
            pl.BlockSpec(memory_space=pltpu.VMEM),
            pl.BlockSpec(memory_space=pltpu.VMEM),
            pl.BlockSpec(memory_space=pltpu.VMEM),
            pl.BlockSpec(memory_space=pl.ANY),
        ],
        out_specs=pl.BlockSpec(memory_space=pltpu.VMEM),
        scratch_shapes=[
            pltpu.VMEM((levels, 2, sub, width), kind),
            pltpu.VMEM((dps, fs, levels, 2, sub, width), kind),
            pltpu.VMEM((units, width), kind),
            pltpu.VMEM((dps, fs, levels, sub, width), kind),
            pltpu.VMEM((fs, levels, sub, half), kind),
            pltpu.VMEM((dps, fs, sub, half), kind),
            pltpu.VMEM((fs, sub, width), kind),
            pltpu.VMEM((dps, fs, levels, sub, width), kind),
            pltpu.VMEM((dps - 1, fs, levels, sub, half), kind),
            pltpu.VMEM((levels - 1, dps, fs, sub, half), kind),
            pltpu.VMEM((levels - 1, fs, sub, half), kind),
            pltpu.VMEM((dps - 1, fs, sub, half), kind),
            pltpu.VMEM((fs - 1, sub, width), kind),
            pltpu.SemaphoreType.DMA((sems,)),
            pltpu.SemaphoreType.DMA((sems,)),
            pltpu.SemaphoreType.DMA((pieces,)),
        ],
        compiler_params=pltpu.CompilerParams(
            collective_id=number, has_side_effects=True, vmem_limit_bytes=56 << 20
        ),
        name="collect",
    )(hidden, share, residual, down_weight)


def local(
    sizes,
    window,
    attention_gain,
    query_weight,
    key_weight,
    value_weight,
    out_weight,
    cache_keys,
    cache_values,
    occluded,
    feedforward_gain,
    router_weight,
    chosen_experts,
    gate_weight,
    up_weight,
    down_weight,
):
    dps, fs, es = sizes["dp"], sizes["fsdp"], sizes["expert"]
    token_rows, width = window.shape
    d, f, e = lax.axis_index("dp"), lax.axis_index("fsdp"), lax.axis_index("expert")
    query_width = query_weight.shape[1]
    key_width = key_weight.shape[1]
    query_heads = query_width // HD
    key_heads = key_width // HD
    grouping = query_heads // key_heads
    window_rows = token_rows * fs
    prefix_rows = cache_keys.shape[0] * dps
    score_scale = HD ** (-0.5)
    part = token_rows // dps
    sub = token_rows // es

    own_rows = lax.dynamic_slice_in_dim(window, d * part, part, 0)
    normed = rms_norm(own_rows, attention_gain)
    flags = occluded.astype(jnp.float32).T
    columns, keys_block = exchange(
        sizes, 0, (normed, "columns", ("fsdp",)), (cache_keys, "gather", ("dp",))
    )
    columns = columns.reshape(fs * part, width // fs)
    sums = jnp.concatenate(
        [
            jnp.dot(columns, weight, preferred_element_type=jnp.float32)
            for weight in (query_weight, key_weight, value_weight)
        ],
        axis=1,
    )
    sums, values_block, flags_block = exchange(
        sizes,
        1,
        (sums.reshape(fs, part, -1), "rows", ("fsdp",)),
        (cache_values, "gather", ("dp",)),
        (flags, "gather", ("dp",)),
    )
    sums = jnp.sum(sums, axis=0)
    positions = prefix_rows + f * token_rows + d * part + jnp.arange(part, dtype=jnp.int32)
    rotated = rotate(
        sums[:, : query_width + key_width].reshape(part, query_heads + key_heads, HD), positions
    ).astype(jnp.bfloat16)
    queries = rotated[:, :query_heads].reshape(part, query_width)
    fresh = jnp.concatenate(
        [
            rotated[:, query_heads:].reshape(part, key_width),
            sums[:, query_width + key_width :].astype(jnp.bfloat16),
        ],
        axis=1,
    )
    queries, fresh = exchange(
        sizes, 2, (queries, "gather", ("dp",)), (fresh, "gather", ("fsdp", "dp"))
    )
    fresh = fresh.reshape(window_rows, 2 * key_width)
    query_grid = queries.reshape(token_rows, key_heads, grouping, HD)
    all_keys = jnp.concatenate(
        [keys_block.reshape(prefix_rows, key_width), fresh[:, :key_width]], axis=0
    ).reshape(prefix_rows + window_rows, key_heads, HD)
    all_values = jnp.concatenate(
        [values_block.reshape(prefix_rows, key_width), fresh[:, key_width:]], axis=0
    ).reshape(prefix_rows + window_rows, key_heads, HD)
    scores = (
        jnp.einsum("tkgd,nkd->kgtn", query_grid, all_keys, preferred_element_type=jnp.float32)
        * score_scale
    )
    seen = lax.dynamic_slice_in_dim(flags_block, d, 1, 1).reshape(prefix_rows) == 0
    causal = (
        jnp.arange(window_rows)[None, :]
        <= (f * token_rows + jnp.arange(token_rows))[:, None]
    )
    visible = jnp.concatenate(
        [jnp.broadcast_to(seen[None, :], (token_rows, prefix_rows)), causal], axis=1
    )
    masked = jnp.where(visible, scores, floor_score)
    top = jnp.max(masked, axis=-1, keepdims=True)
    weights = jnp.exp(masked - top)
    totals = jnp.sum(weights, axis=-1)
    heads = jnp.einsum(
        "kgtn,nkd->tkgd",
        weights.astype(jnp.bfloat16),
        all_values,
        preferred_element_type=jnp.float32,
    ) / totals.transpose(2, 0, 1)[..., None]
    attended = heads.reshape(token_rows, query_width).astype(jnp.bfloat16)

    projected = project(sizes, 3, attended, out_weight, sub)
    residual = lax.dynamic_slice_in_dim(window, e * sub, sub, 0).astype(jnp.float32) + projected
    normed_mix = rms_norm(residual, feedforward_gain)
    logits = jnp.dot(normed_mix, router_weight, preferred_element_type=jnp.float32)
    picks = lax.dynamic_slice_in_dim(chosen_experts.reshape(token_rows, TOP), e * sub, sub, 0)
    experts = router_weight.shape[1]
    matches = picks[:, :, None] == jnp.arange(experts, dtype=jnp.int32)[None, None, :]
    picked = jnp.sum(jnp.where(matches, logits[:, None, :], 0.0), axis=-1)
    gate_shares = jax.nn.sigmoid(picked - picked[:, ::-1])
    lanes = picks[:, :, None] == jnp.arange(128, dtype=jnp.int32)[None, None, :]
    shares = jnp.sum(jnp.where(lanes, gate_shares[:, :, None], 0.0), axis=1)

    hidden, shares = spread(sizes, 6, normed_mix, shares, gate_weight, up_weight)
    share = lax.dynamic_slice_in_dim(shares.reshape(dps * window_rows, 128), e, 1, 1)
    whole = collect(sizes, 7, hidden, share, residual, down_weight)
    return whole.reshape(1, token_rows, width)


def solution(mesh):
    sizes = dict(mesh.shape)
    placed = (
        P("fsdp", None),
        P(),
        P("fsdp", "expert"),
        P("fsdp", "expert"),
        P("fsdp", "expert"),
        P("expert", "fsdp"),
        P("dp", "expert"),
        P("dp", "expert"),
        P("dp", None),
        P(),
        P(),
        P("dp", "fsdp", None),
        P("expert", ("dp", "fsdp"), None),
        P("expert", ("dp", "fsdp"), None),
        P("expert", ("dp", "fsdp"), None),
    )
    return jax.shard_map(
        functools.partial(local, sizes),
        mesh=mesh,
        in_specs=placed,
        out_specs=P("dp", "fsdp", None),
        check_vma=False,
    )
```
